128 devices in a mesh: room: 4 (over x_hi, core), geom: 32 (over z, x_lo, y).
Axes of the slice: x: 4 (x_hi: 2, x_lo: 2; x = x_hi * 2 + x_lo), y: 4, z: 4, core: 2. Of those that a mesh axis runs over, the one named last changes fastest.
Arguments:
- queries: bfloat16 [4, 4096, 512], P('room', 'geom'), may hold values from -6 to 6
- features: bfloat16 [4, 4096, 512], P('room', 'geom'), may hold values from -45 to 45
- visible: int32 [4, 32, 32], P('room', 'geom'), may hold values from 0 to 1, as said below
- cotangent: bfloat16 [4, 4096, 512], P('room', 'geom'), may hold values from -0.125 to 0.125
- w_query: bfloat16 [512, 512], replicated, may hold values from -0.25 to 0.25
- w_key: bfloat16 [512, 512], replicated, may hold values from -0.25 to 0.25
- w_value: bfloat16 [512, 512], replicated, may hold values from -0.25 to 0.25
- w_out: bfloat16 [512, 512], replicated, may hold values from -0.25 to 0.25
- w_up: bfloat16 [512, 1024], replicated, may hold values from -0.25 to 0.25
- w_down: bfloat16 [1024, 512], replicated, may hold values from -0.1875 to 0.1875
- gain_attn: float32 [512], replicated, may hold values from 0.25 to 1.75
- gain_mlp: float32 [512], replicated, may hold values from 0.25 to 1.75
Outputs:
- output: bfloat16 [4, 4096, 512], P('room', 'geom')
- grad_query_w: bfloat16 [512, 512], replicated
- grad_key_w: bfloat16 [512, 512], replicated
- grad_value_w: bfloat16 [512, 512], replicated
- grad_out_w: bfloat16 [512, 512], replicated
- grad_up_w: bfloat16 [512, 1024], replicated
- grad_down_w: bfloat16 [1024, 512], replicated
- grad_gain_attn: bfloat16 [512], replicated
- grad_gain_mlp: bfloat16 [512], replicated
The draws below stay inside these ranges and needn't reach their ends.
Inputs may be any that keep to these rules, and one draw needn't show every extreme that they name: `visible`: every query block sees at least one key block.
All inputs are finite; a program needn't handle non-finite values.
Results may differ from the reference program's by a relative error of at most 0.017.
The reference program's roundings to bfloat16 on the way count: a program that leaves them out, or rounds other values in their place, can miss the bound.
Values may be sent and summed in bfloat16 or wider, within the bound.
No kernel may reach another device: no remote copies, remote signals or barrier semaphores. Data moves between devices by JAX's collectives and lax.ppermute only.
A program may use at most 128 MiB of HBM per device.

```python
import math
import jax
import jax.numpy as jnp
from jax import lax

D = 512
HEADS = 4
F = 1024
BLK = 128
FEAT = 4096
Q_DEV = 128
ROOMS = 4
QTOK = 4096
QBLK = 32
KBLK = 32
N_GEOM = 32


def draw_features(key, part):
    shape = (ROOMS, FEAT, D)
    base = jax.random.normal(key, shape, jnp.float32)
    return jnp.clip(base, -6.0, 6.0).astype(jnp.bfloat16)


def draw_visible(key, part):
    first = jax.random.fold_in(key, 11)
    second = jax.random.fold_in(key, 23)
    offset = jax.random.randint(first, (ROOMS, QBLK, 1), 0, KBLK)
    count = jax.random.randint(second, (ROOMS, QBLK, 1), 1, KBLK + 1)
    blocks = jnp.arange(KBLK, dtype=jnp.int32)[None, None, :]
    return ((blocks - offset) % KBLK < count).astype(jnp.int32)


def steps_of(own_key, extent, cuts, low, top_value):
    def one(axis_at, blocks):
        draws = jax.random.uniform(jax.random.fold_in(jax.random.fold_in(own_key, 6), axis_at), (blocks,), jnp.float32, low / len(cuts), top_value / len(cuts))
        return jnp.repeat(jnp.exp(draws), extent[axis_at] // blocks).reshape((-1,) + (1,) * (len(extent) - axis_at - 1))

    factor_of = one(*cuts[0])
    for cut in cuts[1:]:
        factor_of = factor_of * one(*cut)
    return factor_of


def noise(own_key, shape, deviation, reach, cuts=(), held_as=jnp.bfloat16):
    result = deviation * jax.random.normal(own_key, shape, jnp.float32)
    if cuts:
        result = result * steps_of(own_key, shape, cuts, -0.22, 0.18)
    return jnp.clip(result, -reach, reach).astype(held_as)


def setup_inputs(seed: int = 0) -> dict:
    key_of = jax.random.split(jax.random.key(seed), 13)
    queries = noise(key_of[0], (ROOMS, QTOK, D), 1.0, 6.0, ((0, 4), (1, 32)))
    features = draw_features(jax.random.fold_in(key_of[12], 71), 0)
    visible = draw_visible(jax.random.fold_in(key_of[12], 71), 0)
    cotangent = noise(key_of[3], (ROOMS, QTOK, D), (1.0 / (ROOMS * QTOK) ** 0.5), 0.125, ((0, 4), (1, 32)))
    w_query = noise(key_of[4], (D, D), D ** -0.5, 0.25)
    w_key = noise(key_of[5], (D, D), D ** -0.5, 0.25)
    w_value = noise(key_of[6], (D, D), D ** -0.5, 0.25)
    w_out = noise(key_of[7], (D, D), D ** -0.5, 0.25)
    w_up = noise(key_of[8], (D, F), D ** -0.5, 0.25)
    w_down = noise(key_of[9], (F, D), F ** -0.5, 0.1875)
    gain_attn = jnp.clip(1.0 + 0.15 * jax.random.normal(key_of[10], (D,), jnp.float32), 0.25, 1.75)
    gain_mlp = jnp.clip(1.0 + 0.15 * jax.random.normal(key_of[11], (D,), jnp.float32), 0.25, 1.75)
    return {"queries": queries, "features": features, "visible": visible, "cotangent": cotangent, "w_query": w_query, "w_key": w_key, "w_value": w_value, "w_out": w_out, "w_up": w_up, "w_down": w_down, "gain_attn": gain_attn, "gain_mlp": gain_mlp}


EPSILON = 1e-05
GELU_COEF = math.sqrt(2.0 / math.pi)

def normalize(inputs, gain):
    center = inputs - lax.optimization_barrier(jnp.mean(inputs, axis=-1, keepdims=True))
    inverse = lax.rsqrt(lax.optimization_barrier(jnp.mean(center * center, axis=-1, keepdims=True)) + EPSILON)
    scaled = center * inverse
    return (scaled, inverse, scaled * gain)

def gelu_pair(inputs):
    inner = GELU_COEF * (inputs + 0.044715 * inputs * inputs * inputs)
    tangent = jnp.tanh(inner)
    value = 0.5 * inputs * (1.0 + tangent)
    slope = 0.5 * (1.0 + tangent) + 0.5 * inputs * (1.0 - tangent * tangent) * GELU_COEF * (1.0 + 3.0 * 0.044715 * inputs * inputs)
    return (value, slope)

def mult_nt(left, right):
    return lax.dot_general(left, right, (((1,), (1,)), ((), ())), preferred_element_type=jnp.float32)

def mult_tn(left, right):
    return lax.dot_general(left, right, (((0,), (0,)), ((), ())), preferred_element_type=jnp.float32)

def device_step(queries, visible, cotangent, key_rows, value_rows, w_query, w_out, w_up, w_down, gain_attn, gain_mlp):
    head_size = key_rows.shape[1] // HEADS
    factor = 1.0 / math.sqrt(head_size)
    allowed = jnp.repeat(jnp.repeat(visible > 0, BLK, axis=0), BLK, axis=1)
    inputs = queries.astype(jnp.float32)
    scaled_one, inverse_one, normed = normalize(inputs, gain_attn)
    normed_b = normed.astype(jnp.bfloat16)
    query_rows = jnp.dot(normed_b, w_query, preferred_element_type=jnp.float32).astype(jnp.bfloat16)
    contexts = []
    saved = []
    for head_index in range(HEADS):
        lower = head_index * head_size
        query_head = query_rows[:, lower:lower + head_size]
        key_head = key_rows[:, lower:lower + head_size]
        value_head = value_rows[:, lower:lower + head_size]
        scores = mult_nt(query_head, key_head) * factor
        scores = jnp.where(allowed, scores, -1e+30)
        highest = lax.optimization_barrier(jnp.max(scores, axis=-1, keepdims=True))
        expo = jnp.exp(scores - highest)
        attend = expo / lax.optimization_barrier(jnp.sum(expo, axis=-1, keepdims=True))
        attend_b = attend.astype(jnp.bfloat16)
        contexts.append(jnp.dot(attend_b, value_head, preferred_element_type=jnp.float32).astype(jnp.bfloat16))
        saved.append((attend, attend_b))
    context = jnp.concatenate(contexts, axis=1)
    mixed = inputs + jnp.dot(context, w_out, preferred_element_type=jnp.float32)
    scaled_two, inverse_two, normed_two = normalize(mixed, gain_mlp)
    normed_two_b = normed_two.astype(jnp.bfloat16)
    upper = jnp.dot(normed_two_b, w_up, preferred_element_type=jnp.float32)
    activated, slope = gelu_pair(upper)
    activated_b = activated.astype(jnp.bfloat16)
    output = (mixed + jnp.dot(activated_b, w_down, preferred_element_type=jnp.float32)).astype(jnp.bfloat16)
    grad_down = mult_tn(activated_b, cotangent)
    grad_activated = mult_nt(cotangent, w_down)
    grad_upper_b = (grad_activated * slope).astype(jnp.bfloat16)
    grad_up = mult_tn(normed_two_b, grad_upper_b)
    grad_normed_two = mult_nt(grad_upper_b, w_up)
    grad_gain_mlp = lax.optimization_barrier(jnp.sum(grad_normed_two * scaled_two, axis=0))
    grad_scaled = grad_normed_two * gain_mlp
    mean_one = lax.optimization_barrier(jnp.mean(grad_scaled, axis=-1, keepdims=True))
    mean_two = lax.optimization_barrier(jnp.mean(grad_scaled * scaled_two, axis=-1, keepdims=True))
    grad_mixed = cotangent.astype(jnp.float32) + inverse_two * (grad_scaled - mean_one - scaled_two * mean_two)
    grad_mixed_b = grad_mixed.astype(jnp.bfloat16)
    grad_out = mult_tn(context, grad_mixed_b)
    grad_context = mult_nt(grad_mixed_b, w_out).astype(jnp.bfloat16)
    grad_queries = []
    grad_keys = []
    grad_values = []
    for head_index in range(HEADS):
        lower = head_index * head_size
        query_head = query_rows[:, lower:lower + head_size]
        key_head = key_rows[:, lower:lower + head_size]
        value_head = value_rows[:, lower:lower + head_size]
        attend, attend_b = saved[head_index]
        grad_head = grad_context[:, lower:lower + head_size]
        grad_attend = mult_nt(grad_head, value_head)
        grad_values.append(mult_tn(attend_b, grad_head))
        centre = lax.optimization_barrier(jnp.sum(attend * grad_attend, axis=-1, keepdims=True))
        grad_scores = (attend * (grad_attend - centre) * factor).astype(jnp.bfloat16)
        grad_queries.append(jnp.dot(grad_scores, key_head, preferred_element_type=jnp.float32))
        grad_keys.append(mult_tn(grad_scores, query_head))
    grad_query_rows = jnp.concatenate(grad_queries, axis=1).astype(jnp.bfloat16)
    partial_keys = jnp.concatenate(grad_keys, axis=1).astype(jnp.bfloat16)
    partial_values = jnp.concatenate(grad_values, axis=1).astype(jnp.bfloat16)
    grad_query = mult_tn(normed_b, grad_query_rows)
    grad_normed = mult_nt(grad_query_rows, w_query)
    grad_gain_attn = lax.optimization_barrier(jnp.sum(grad_normed * scaled_one, axis=0))
    grads = (grad_query, grad_out, grad_up, grad_down, grad_gain_attn, grad_gain_mlp)
    return (output, grads, partial_keys, partial_values)

def reference(queries, features, visible, cotangent, w_query, w_key, w_value, w_out, w_up, w_down, gain_attn, gain_mlp):
    width = w_query.shape[0]
    hidden = w_up.shape[1]
    totals = (jnp.zeros((width, width), jnp.float32), jnp.zeros((width, width), jnp.float32), jnp.zeros((width, hidden), jnp.float32), jnp.zeros((hidden, width), jnp.float32), jnp.zeros((width,), jnp.float32), jnp.zeros((width,), jnp.float32))
    key_total = jnp.zeros((width, width), jnp.float32)
    value_total = jnp.zeros((width, width), jnp.float32)
    outputs = []
    for room_index in range(ROOMS):
        feature_room = features[room_index]
        key_rows = jnp.dot(feature_room, w_key, preferred_element_type=jnp.float32).astype(jnp.bfloat16)
        value_rows = jnp.dot(feature_room, w_value, preferred_element_type=jnp.float32).astype(jnp.bfloat16)
        query_groups = queries[room_index].reshape(N_GEOM, Q_DEV, width)
        cot_groups = cotangent[room_index].reshape(N_GEOM, Q_DEV, width)
        vis_groups = visible[room_index].reshape(N_GEOM, Q_DEV // BLK, visible.shape[2])

        def group_step(carry, pieces):
            sums, key_sum, value_sum = carry
            output, grads, partial_keys, partial_values = device_step(pieces[0], pieces[1], pieces[2], key_rows, value_rows, w_query, w_out, w_up, w_down, gain_attn, gain_mlp)
            sums = tuple((left + right for left, right in zip(sums, grads)))
            return ((sums, key_sum + partial_keys.astype(jnp.float32), value_sum + partial_values.astype(jnp.float32)), output)
        start = (totals, jnp.zeros((FEAT, width), jnp.float32), jnp.zeros((FEAT, width), jnp.float32))
        (totals, key_sum, value_sum), room_out = lax.scan(group_step, start, (query_groups, vis_groups, cot_groups))
        feature_f = feature_room.astype(jnp.float32)
        key_total = key_total + jnp.dot(feature_f.T, key_sum, precision=lax.Precision.HIGHEST)
        value_total = value_total + jnp.dot(feature_f.T, value_sum, precision=lax.Precision.HIGHEST)
        outputs.append(room_out.reshape(N_GEOM * Q_DEV, width))
    output = jnp.stack(outputs, axis=0)
    grad_query, grad_out, grad_up, grad_down, grad_gain_attn, grad_gain_mlp = totals
    return (output, grad_query.astype(jnp.bfloat16), key_total.astype(jnp.bfloat16), value_total.astype(jnp.bfloat16), grad_out.astype(jnp.bfloat16), grad_up.astype(jnp.bfloat16), grad_down.astype(jnp.bfloat16), grad_gain_attn.astype(jnp.bfloat16), grad_gain_mlp.astype(jnp.bfloat16))
```

```python
import math

import jax
import jax.numpy as jnp
from jax import lax
from jax.sharding import Mesh, PartitionSpec as P

HEADS = 4
BLK = 128
EPSILON = 1e-05
GELU_COEF = math.sqrt(2.0 / math.pi)

AXES = ("x_hi", "core", "z", "x_lo", "y")
ROOM = ("x_hi", "core")
GEOM = ("z", "x_lo", "y")


def normalize(inputs, gain):
    center = inputs - jnp.mean(inputs, axis=-1, keepdims=True)
    inverse = lax.rsqrt(jnp.mean(center * center, axis=-1, keepdims=True) + EPSILON)
    scaled = center * inverse
    return (scaled, inverse, scaled * gain)


def gelu_pair(inputs):
    inner = GELU_COEF * (inputs + 0.044715 * inputs * inputs * inputs)
    tangent = jnp.tanh(inner)
    value = 0.5 * inputs * (1.0 + tangent)
    slope = 0.5 * (1.0 + tangent) + 0.5 * inputs * (1.0 - tangent * tangent) * GELU_COEF * (
        1.0 + 3.0 * 0.044715 * inputs * inputs
    )
    return (value, slope)


def mult(left, right):
    return jnp.dot(left, right, preferred_element_type=jnp.float32)


def mult_nt(left, right):
    return lax.dot_general(
        left, right, (((1,), (1,)), ((), ())), preferred_element_type=jnp.float32
    )


def mult_tn(left, right):
    return lax.dot_general(
        left, right, (((0,), (0,)), ((), ())), preferred_element_type=jnp.float32
    )


def two_parts(value):
    high = value.astype(jnp.bfloat16)
    low = (value - high.astype(jnp.float32)).astype(jnp.bfloat16)
    return high, low


def device_step(
    queries,
    visible,
    cotangent,
    feats,
    w_query,
    w_key,
    w_value,
    w_out,
    w_up,
    w_down,
    gain_attn,
    gain_mlp,
):
    head = w_query.shape[1] // HEADS
    rows = queries.shape[0]
    factor = 1.0 / math.sqrt(head)
    allowed = jnp.repeat(jnp.repeat(visible > 0, BLK, axis=0), BLK, axis=1)
    inputs = queries.astype(jnp.float32)
    scaled_one, _, normed = normalize(inputs, gain_attn)
    normed_b = normed.astype(jnp.bfloat16)
    query_rows = mult(normed_b, w_query).astype(jnp.bfloat16)
    key_rows = mult(feats, w_key).astype(jnp.bfloat16)
    cols = [slice(h * head, (h + 1) * head) for h in range(HEADS)]
    scores = []
    for c in cols:
        part = mult_nt(query_rows[:, c], key_rows[:, c]) * factor
        scores.append(jnp.where(allowed, part, -1e30))
    scores = jnp.concatenate(scores, axis=0)
    expo = jnp.exp(scores - jnp.max(scores, axis=-1, keepdims=True))
    attend = expo / jnp.sum(expo, axis=-1, keepdims=True)
    attend_b = attend.astype(jnp.bfloat16)
    u_high, u_low = two_parts(mult(attend_b, feats))
    heads = [slice(h * rows, (h + 1) * rows) for h in range(HEADS)]
    context = jnp.concatenate(
        [mult(u_high[r], w_value[:, c]) + mult(u_low[r], w_value[:, c]) for r, c in zip(heads, cols)],
        axis=1,
    ).astype(jnp.bfloat16)
    mixed = inputs + mult(context, w_out)
    scaled_two, inverse_two, normed_two = normalize(mixed, gain_mlp)
    normed_two_b = normed_two.astype(jnp.bfloat16)
    activated, slope = gelu_pair(mult(normed_two_b, w_up))
    activated_b = activated.astype(jnp.bfloat16)
    output = (mixed + mult(activated_b, w_down)).astype(jnp.bfloat16)
    grad_down = mult_tn(activated_b, cotangent)
    grad_upper_b = (mult_nt(cotangent, w_down) * slope).astype(jnp.bfloat16)
    grad_up = mult_tn(normed_two_b, grad_upper_b)
    grad_normed_two = mult_nt(grad_upper_b, w_up)
    grad_gain_mlp = jnp.sum(grad_normed_two * scaled_two, axis=0)
    grad_scaled = grad_normed_two * gain_mlp
    mean_one = jnp.mean(grad_scaled, axis=-1, keepdims=True)
    mean_two = jnp.mean(grad_scaled * scaled_two, axis=-1, keepdims=True)
    grad_mixed = cotangent.astype(jnp.float32) + inverse_two * (
        grad_scaled - mean_one - scaled_two * mean_two
    )
    grad_mixed_b = grad_mixed.astype(jnp.bfloat16)
    grad_out = mult_tn(context, grad_mixed_b)
    grad_context = mult_nt(grad_mixed_b, w_out).astype(jnp.bfloat16)
    grad_value = jnp.concatenate(
        [
            mult_tn(u_high[r], grad_context[:, c]) + mult_tn(u_low[r], grad_context[:, c])
            for r, c in zip(heads, cols)
        ],
        axis=1,
    )
    pulled = jnp.concatenate(
        [mult_nt(grad_context[:, c], w_value[:, c]) for c in cols], axis=0
    ).astype(jnp.bfloat16)
    grad_attend = mult_nt(pulled, feats)
    centre = jnp.sum(attend * grad_attend, axis=-1, keepdims=True)
    grad_scores = (attend * (grad_attend - centre) * factor).astype(jnp.bfloat16)
    t_high, t_low = two_parts(mult(grad_scores, feats))
    grad_query_rows = jnp.concatenate(
        [mult(t_high[r], w_key[:, c]) + mult(t_low[r], w_key[:, c]) for r, c in zip(heads, cols)],
        axis=1,
    ).astype(jnp.bfloat16)
    grad_key = jnp.concatenate(
        [
            mult_tn(t_high[r], query_rows[:, c]) + mult_tn(t_low[r], query_rows[:, c])
            for r, c in zip(heads, cols)
        ],
        axis=1,
    )
    grad_query = mult_tn(normed_b, grad_query_rows)
    grad_normed = mult_nt(grad_query_rows, w_query)
    grad_gain_attn = jnp.sum(grad_normed * scaled_one, axis=0)
    return output, (
        grad_query,
        grad_key,
        grad_value,
        grad_out,
        grad_up,
        grad_down,
        grad_gain_attn,
        grad_gain_mlp,
    )


def local(
    queries,
    features,
    visible,
    cotangent,
    w_query,
    w_key,
    w_value,
    w_out,
    w_up,
    w_down,
    gain_attn,
    gain_mlp,
):
    own = features[0]
    many = visible.shape[-1]
    feats = lax.all_to_all(
        jnp.broadcast_to(own[None], (many,) + own.shape), GEOM, 0, 0, tiled=True
    ).reshape(many * own.shape[0], own.shape[1])
    output, grads = device_step(
        queries[0],
        visible[0],
        cotangent[0],
        feats,
        w_query,
        w_key,
        w_value,
        w_out,
        w_up,
        w_down,
        gain_attn,
        gain_mlp,
    )
    totals = lax.psum(grads, AXES)
    return (output[None],) + tuple(piece.astype(jnp.bfloat16) for piece in totals)


def solution(mesh):
    parts = Mesh(mesh.devices.reshape(2, 2, 4, 2, 4), AXES)
    split = P(ROOM, GEOM, None)
    return jax.shard_map(
        local,
        mesh=parts,
        in_specs=(split,) * 4 + (P(),) * 8,
        out_specs=(split,) + (P(),) * 8,
        check_vma=False,
    )
```

```python
import math

import jax
import jax.numpy as jnp
import numpy as np
from jax import lax
from jax.experimental import pallas as pl
from jax.experimental.pallas import tpu as pltpu
from jax.sharding import Mesh, PartitionSpec as P

HEADS = 4
BLK = 128
EPSILON = 1e-05
GELU_COEF = math.sqrt(2.0 / math.pi)

AXES = ("x_hi", "core", "z", "x_lo", "y")
SIZES = (2, 2, 4, 2, 4)
ROOM = ("x_hi", "core")
GEOM = ("z", "x_lo", "y")
VMEM = pl.BlockSpec(memory_space=pltpu.VMEM)
SMEM = pl.BlockSpec(memory_space=pltpu.SMEM)


def pairs_of(move):
    pairs = []
    for source in range(math.prod(SIZES)):
        target = move(*(int(i) for i in np.unravel_index(source, SIZES)))
        pairs.append((source, int(np.ravel_multi_index(target, SIZES))))
    return pairs


SWAP = pairs_of(lambda xh, c, z, xl, y: (xh, xl, z, c, y))
CORE = pairs_of(lambda xh, c, z, xl, y: (xh, 1 - c, z, xl, y))


def first(mask):
    return pairs_of(
        lambda xh, c, z, xl, y: (xh, c, z, xl, y ^ mask) if c == 0 else (xh, c, z ^ mask, xl, y)
    )


def second(mask):
    return pairs_of(
        lambda xh, c, z, xl, y: (xh, c, z ^ mask, xl, y) if c == 0 else (xh, c, z, xl, y ^ mask)
    )


def along_x(mask):
    return pairs_of(lambda xh, c, z, xl, y: (xh ^ (mask >> 1), c, z, xl ^ (mask & 1), y))


def send(value, pairs):
    return lax.ppermute(value, AXES, pairs)


def normalize(inputs, gain):
    center = inputs - jnp.mean(inputs, axis=-1, keepdims=True)
    inverse = lax.rsqrt(jnp.mean(center * center, axis=-1, keepdims=True) + EPSILON)
    scaled = center * inverse
    return (scaled, inverse, scaled * gain)


def gelu_pair(inputs):
    inner = GELU_COEF * (inputs + 0.044715 * inputs * inputs * inputs)
    tangent = jnp.tanh(inner)
    value = 0.5 * inputs * (1.0 + tangent)
    slope = 0.5 * (1.0 + tangent) + 0.5 * inputs * (1.0 - tangent * tangent) * GELU_COEF * (
        1.0 + 3.0 * 0.044715 * inputs * inputs
    )
    return (value, slope)


def mult(left, right):
    return jnp.dot(left, right, preferred_element_type=jnp.float32)


def mult_nt(left, right):
    return lax.dot_general(
        left, right, (((1,), (1,)), ((), ())), preferred_element_type=jnp.float32
    )


def mult_tn(left, right):
    return lax.dot_general(
        left, right, (((0,), (0,)), ((), ())), preferred_element_type=jnp.float32
    )


def two_parts(value):
    high = value.astype(jnp.bfloat16)
    low = (value - high.astype(jnp.float32)).astype(jnp.bfloat16)
    return high, low


def device_step(
    queries,
    visible,
    cotangent,
    feats,
    w_query,
    w_key,
    w_value,
    w_out,
    w_up,
    w_down,
    gain_attn,
    gain_mlp,
):
    head = w_query.shape[1] // HEADS
    rows = queries.shape[0]
    factor = 1.0 / math.sqrt(head)
    allowed = jnp.repeat(visible > 0, BLK)[None, :]
    inputs = queries.astype(jnp.float32)
    scaled_one, _, normed = normalize(inputs, gain_attn)
    normed_b = normed.astype(jnp.bfloat16)
    query_rows = mult(normed_b, w_query).astype(jnp.bfloat16)
    key_rows = mult(feats, w_key).astype(jnp.bfloat16)
    cols = [slice(h * head, (h + 1) * head) for h in range(HEADS)]
    scores = []
    for c in cols:
        part = mult_nt(query_rows[:, c], key_rows[:, c]) * factor
        scores.append(jnp.where(allowed, part, -1e30))
    scores = jnp.concatenate(scores, axis=0)
    expo = jnp.exp(scores - jnp.max(scores, axis=-1, keepdims=True))
    attend = expo / jnp.sum(expo, axis=-1, keepdims=True)
    attend_b = attend.astype(jnp.bfloat16)
    u_high, u_low = two_parts(mult(attend_b, feats))
    heads = [slice(h * rows, (h + 1) * rows) for h in range(HEADS)]
    context = jnp.concatenate(
        [mult(u_high[r], w_value[:, c]) + mult(u_low[r], w_value[:, c]) for r, c in zip(heads, cols)],
        axis=1,
    ).astype(jnp.bfloat16)
    mixed = inputs + mult(context, w_out)
    scaled_two, inverse_two, normed_two = normalize(mixed, gain_mlp)
    normed_two_b = normed_two.astype(jnp.bfloat16)
    activated, slope = gelu_pair(mult(normed_two_b, w_up))
    activated_b = activated.astype(jnp.bfloat16)
    output = (mixed + mult(activated_b, w_down)).astype(jnp.bfloat16)
    grad_down = mult_tn(activated_b, cotangent)
    grad_upper_b = (mult_nt(cotangent, w_down) * slope).astype(jnp.bfloat16)
    grad_up = mult_tn(normed_two_b, grad_upper_b)
    grad_normed_two = mult_nt(grad_upper_b, w_up)
    grad_gain_mlp = jnp.sum(grad_normed_two * scaled_two, axis=0)
    grad_scaled = grad_normed_two * gain_mlp
    mean_one = jnp.mean(grad_scaled, axis=-1, keepdims=True)
    mean_two = jnp.mean(grad_scaled * scaled_two, axis=-1, keepdims=True)
    grad_mixed = cotangent.astype(jnp.float32) + inverse_two * (
        grad_scaled - mean_one - scaled_two * mean_two
    )
    grad_mixed_b = grad_mixed.astype(jnp.bfloat16)
    grad_out = mult_tn(context, grad_mixed_b)
    grad_context = mult_nt(grad_mixed_b, w_out).astype(jnp.bfloat16)
    grad_value = jnp.concatenate(
        [
            mult_tn(u_high[r], grad_context[:, c]) + mult_tn(u_low[r], grad_context[:, c])
            for r, c in zip(heads, cols)
        ],
        axis=1,
    )
    pulled = jnp.concatenate(
        [mult_nt(grad_context[:, c], w_value[:, c]) for c in cols], axis=0
    ).astype(jnp.bfloat16)
    grad_attend = mult_nt(pulled, feats)
    centre = jnp.sum(attend * grad_attend, axis=-1, keepdims=True)
    grad_scores = (attend * (grad_attend - centre) * factor).astype(jnp.bfloat16)
    t_high, t_low = two_parts(mult(grad_scores, feats))
    grad_query_rows = jnp.concatenate(
        [mult(t_high[r], w_key[:, c]) + mult(t_low[r], w_key[:, c]) for r, c in zip(heads, cols)],
        axis=1,
    ).astype(jnp.bfloat16)
    grad_key = jnp.concatenate(
        [
            mult_tn(t_high[r], query_rows[:, c]) + mult_tn(t_low[r], query_rows[:, c])
            for r, c in zip(heads, cols)
        ],
        axis=1,
    )
    grad_query = mult_tn(normed_b, grad_query_rows)
    grad_normed = mult_nt(grad_query_rows, w_query)
    grad_gain_attn = jnp.sum(grad_normed * scaled_one, axis=0)
    return output, (
        grad_query,
        grad_key,
        grad_value,
        grad_out,
        grad_up,
        grad_down,
        grad_gain_attn,
        grad_gain_mlp,
    )


PIECES = 32
CHUNK = 128
TAIL = 16


def pieces_of(refs, k):
    query, key, value, out, up, down = refs
    rows = pl.ds(pl.multiple_of(k * 16, 16), 16)
    return (
        (0, query.at[rows, :]),
        (16, key.at[rows, :]),
        (32, value.at[rows, :]),
        (48, out.at[rows, :]),
        (64, up.at[rows, pl.ds(0, 512)]),
        (80, up.at[rows, pl.ds(512, 512)]),
        (96, down.at[pl.ds(pl.multiple_of(k * 32, 32), 32), :]),
    )


def put_gains(ref, at, gains):
    high = gains.astype(jnp.bfloat16)
    low = (gains - high.astype(jnp.float32)).astype(jnp.bfloat16)
    ref[at : at + TAIL, :] = jnp.concatenate([high, low], axis=0)


def take_gains(ref, at):
    tail = ref[at : at + TAIL, :].astype(jnp.float32)
    return tail[: TAIL // 2] + tail[TAIL // 2 :]


def halves_kernel(core_ref, *refs):
    grads, gains, give, keep = refs[:6], refs[6], refs[7], refs[8]
    core = core_ref[0]
    half = PIECES // 2

    def step(i, carry):
        row = pl.multiple_of(i * CHUNK, CHUNK)
        for at, piece in pieces_of(grads, (1 - core) * half + i):
            give[pl.ds(row + at, piece.shape[0]), :] = piece[...].astype(jnp.bfloat16)
        for at, piece in pieces_of(grads, core * half + i):
            keep[pl.ds(row + at, piece.shape[0]), :] = piece[...]
        return carry

    lax.fori_loop(0, half, step, 0)
    put_gains(give, half * CHUNK, gains[...])


def quarters_kernel(many, index_ref, own_ref, gains_ref, *refs):
    arrived, gives, keep, gains_out = refs[:many], refs[many : many + 3], refs[many + 3], refs[many + 4]
    index = index_ref[0]
    rows = keep.shape[0]
    total = own_ref.shape[0]
    for mask in range(4):
        at = pl.ds(pl.multiple_of((index ^ mask) * rows, rows), rows)
        value = own_ref[at, :]
        for ref in arrived:
            value = value + ref[at, :].astype(jnp.float32)
        if mask:
            gives[mask - 1][0:rows, :] = value.astype(jnp.bfloat16)
        else:
            keep[...] = value
    gains = add_gains(gains_ref[...], [take_gains(ref, total) for ref in arrived])
    for give in gives:
        put_gains(give, rows, gains)
    gains_out[...] = gains


def add_gains(own, arrived):
    high = own.astype(jnp.bfloat16).astype(jnp.float32)
    own = high + (own - high).astype(jnp.bfloat16).astype(jnp.float32)
    if len(arrived) == 1:
        return own + arrived[0]
    return (own + arrived[0]) + (arrived[1] + arrived[2])


def chunk_kernel(own_ref, gains_ref, *refs):
    arrived, give = refs[:3], refs[3]
    rows = own_ref.shape[0]
    value = own_ref[...]
    for ref in arrived:
        value = value + ref[0:rows, :].astype(jnp.float32)
    give[0:rows, :] = value.astype(jnp.bfloat16)
    put_gains(give, rows, add_gains(gains_ref[...], [take_gains(ref, rows) for ref in arrived]))


def last_kernel(own_ref, *refs):
    arrived, chunk, gains = refs[:3], refs[3], refs[4]
    rows = chunk.shape[0]
    a, b, c, d = (ref[0:rows, :].astype(jnp.float32) for ref in (own_ref, *arrived))
    chunk[...] = ((a + b) + (c + d)).astype(jnp.bfloat16)
    a, b, c, d = (take_gains(ref, rows) for ref in (own_ref, *arrived))
    put_gains(gains, 0, (a + b) + (c + d))


def place_kernel(where_ref, *refs):
    own, other, gains_own, gains_other = refs[0:4], refs[4:8], refs[8], refs[9]
    grads, gains_out = refs[10:16], refs[16]
    core, y, z = where_ref[0], where_ref[1], where_ref[2]
    for side, group in enumerate((own, other)):
        holder = core ^ side
        one = jnp.where(holder == 0, y, z)
        two = jnp.where(holder == 0, z, y)
        for m1 in range(4):
            for m2 in range(4):
                k = holder * 16 + (one ^ m1) * 4 + (two ^ m2)
                for at, piece in pieces_of(grads, k):
                    piece[...] = group[m1][m2 * CHUNK + at : m2 * CHUNK + at + piece.shape[0], :]
    gains = jnp.where(core == 0, take_gains(gains_own, 0), take_gains(gains_other, 0))
    gains_out[...] = gains.astype(jnp.bfloat16)


def call(kernel, outs, *operands, scalars=0):
    return pl.pallas_call(
        kernel,
        out_shape=[jax.ShapeDtypeStruct(shape, dtype) for shape, dtype in outs],
        in_specs=[SMEM] * scalars + [VMEM] * (len(operands) - scalars),
        out_specs=[VMEM] * len(outs),
        compiler_params=pltpu.CompilerParams(vmem_limit_bytes=48 << 20),
    )(*operands)


def sum_everywhere(grads):
    weights, (gain_attn, gain_mlp) = grads[:6], grads[6:]
    core, y, z = (lax.axis_index(name) for name in ("core", "y", "z"))
    gains = jnp.concatenate([gain_attn[None], gain_mlp[None], jnp.zeros((6, 512), jnp.float32)])
    core_at = jnp.asarray(core, jnp.int32).reshape(1)
    one_at = jnp.where(core == 0, y, z).astype(jnp.int32).reshape(1)
    two_at = jnp.where(core == 0, z, y).astype(jnp.int32).reshape(1)
    b16, f32 = jnp.bfloat16, jnp.float32

    give, keep = call(
        halves_kernel,
        [((2048 + TAIL, 512), b16), ((2048, 512), f32)],
        core_at, *weights, gains, scalars=1,
    )
    arrived = [send(give, CORE)]
    for rows, index, route, count in ((512, one_at, first, 1), (128, two_at, second, 3)):
        *gives, keep, gains = call(
            lambda *refs, count=count: quarters_kernel(count, *refs),
            [((rows + TAIL, 512), b16)] * 3 + [((rows, 512), f32), ((8, 512), f32)],
            index, keep, gains, *arrived, scalars=1,
        )
        arrived = [send(give, route(mask)) for mask, give in enumerate(gives, 1)]
    (give,) = call(chunk_kernel, [((128 + TAIL, 512), b16)], keep, gains, *arrived)
    arrived = [send(give, along_x(mask)) for mask in (1, 2, 3)]
    chunk, gains = call(last_kernel, [((128, 512), b16), ((TAIL, 512), b16)], give, *arrived)

    mine = jnp.concatenate([chunk] + [send(chunk, second(mask)) for mask in (1, 2, 3)])
    own = [mine] + [send(mine, first(mask)) for mask in (1, 2, 3)]
    other = [send(part, CORE) for part in own]
    gains_other = send(gains, CORE)
    where = jnp.stack([core, y, z]).astype(jnp.int32)
    *weights, gains = call(
        place_kernel,
        [((512, 512), b16)] * 4 + [((512, 1024), b16), ((1024, 512), b16), ((8, 512), b16)],
        where, *own, *other, gains, gains_other, scalars=1,
    )
    return (*weights, gains[0], gains[1])


def gather_features(own):
    mine = jnp.concatenate([own] + [send(own, first(mask)) for mask in (1, 2, 3)])
    group = [mine] + [send(mine, second(mask)) for mask in (1, 2, 3)]
    parts = group + [send(part, CORE) for part in group]
    core, y, z = (lax.axis_index(name) for name in ("core", "y", "z"))
    side, two, one = (jnp.asarray(i) for i in np.unravel_index(np.arange(32), (2, 4, 4)))
    holder = core ^ side
    block_y = jnp.where(holder == 0, y ^ one, y ^ two)
    block_z = jnp.where(holder == 0, z ^ two, z ^ one)
    return parts, block_z * 8 + holder * 4 + block_y


def local(
    queries,
    features,
    visible,
    cotangent,
    w_query,
    w_key,
    w_value,
    w_out,
    w_up,
    w_down,
    gain_attn,
    gain_mlp,
):
    parts, blocks = gather_features(send(features[0], SWAP))
    moved = send(jnp.concatenate([queries[0], cotangent[0]]), SWAP)
    seen = send(visible[0], SWAP)
    output, grads = device_step(
        moved[:BLK],
        jnp.take(seen[0], blocks),
        moved[BLK:],
        jnp.concatenate(parts),
        w_query,
        w_key,
        w_value,
        w_out,
        w_up,
        w_down,
        gain_attn,
        gain_mlp,
    )
    output = send(output, SWAP)
    return (output[None],) + sum_everywhere(grads)


def solution(mesh):
    parts = Mesh(mesh.devices.reshape(SIZES), AXES)
    split = P(ROOM, GEOM, None)
    return jax.shard_map(
        local,
        mesh=parts,
        in_specs=(split,) * 4 + (P(),) * 8,
        out_specs=(split,) + (P(),) * 8,
        check_vma=False,
    )
```

```python
import math

import jax
import jax.numpy as jnp
import numpy as np
from jax import lax
from jax.experimental import pallas as pl
from jax.experimental.pallas import tpu as pltpu
from jax.sharding import Mesh, PartitionSpec as P

HEADS = 4
BLK = 128
EPSILON = 1e-05
GELU_COEF = math.sqrt(2.0 / math.pi)

AXES = ("x_hi", "core", "z", "x_lo", "y")
SIZES = (2, 2, 4, 2, 4)
ROOM = ("x_hi", "core")
GEOM = ("z", "x_lo", "y")
VMEM = pl.BlockSpec(memory_space=pltpu.VMEM)
SMEM = pl.BlockSpec(memory_space=pltpu.SMEM)


def pairs_of(move):
    pairs = []
    for source in range(math.prod(SIZES)):
        target = move(*(int(i) for i in np.unravel_index(source, SIZES)))
        pairs.append((source, int(np.ravel_multi_index(target, SIZES))))
    return pairs


SWAP = pairs_of(lambda xh, c, z, xl, y: (xh, xl, z, c, y))
CORE = pairs_of(lambda xh, c, z, xl, y: (xh, 1 - c, z, xl, y))


def first(mask):
    return pairs_of(
        lambda xh, c, z, xl, y: (xh, c, z, xl, y ^ mask) if c == 0 else (xh, c, z ^ mask, xl, y)
    )


def second(mask):
    return pairs_of(
        lambda xh, c, z, xl, y: (xh, c, z ^ mask, xl, y) if c == 0 else (xh, c, z, xl, y ^ mask)
    )


def along_x(mask):
    return pairs_of(lambda xh, c, z, xl, y: (xh ^ (mask >> 1), c, z, xl ^ (mask & 1), y))


def send(value, pairs):
    return lax.ppermute(value, AXES, pairs)


def normalize(inputs, gain):
    center = inputs - jnp.mean(inputs, axis=-1, keepdims=True)
    inverse = lax.rsqrt(jnp.mean(center * center, axis=-1, keepdims=True) + EPSILON)
    scaled = center * inverse
    return (scaled, inverse, scaled * gain)


def gelu_pair(inputs):
    inner = GELU_COEF * (inputs + 0.044715 * inputs * inputs * inputs)
    tangent = jnp.tanh(inner)
    value = 0.5 * inputs * (1.0 + tangent)
    slope = 0.5 * (1.0 + tangent) + 0.5 * inputs * (1.0 - tangent * tangent) * GELU_COEF * (
        1.0 + 3.0 * 0.044715 * inputs * inputs
    )
    return (value, slope)


def mult(left, right):
    return jnp.dot(left, right, preferred_element_type=jnp.float32)


def mult_nt(left, right):
    return lax.dot_general(
        left, right, (((1,), (1,)), ((), ())), preferred_element_type=jnp.float32
    )


def mult_tn(left, right):
    return lax.dot_general(
        left, right, (((0,), (0,)), ((), ())), preferred_element_type=jnp.float32
    )


def two_parts(value):
    high = value.astype(jnp.bfloat16)
    low = (value - high.astype(jnp.float32)).astype(jnp.bfloat16)
    return high, low


PARTS = 8
def lanes(value, combine):
    out = value[:, 0:BLK]
    for at in range(BLK, value.shape[1], BLK):
        out = combine(out, value[:, at : at + BLK])
    return out


def step_kernel(core_ref, moved, seen, w_query, w_key, w_value, w_out, w_up, w_down, gain_attn, gain_mlp, *refs):
    parts, (output, give, keep, gains_out) = refs[:PARTS], refs[PARTS : PARTS + 4]
    feats, scores, pulls, sums, stat, sems = refs[PARTS + 4 :]
    f32, b16 = jnp.float32, jnp.bfloat16
    copies = [pltpu.make_async_copy(parts[p], feats.at[p], sems.at[p]) for p in range(PARTS)]
    for copy in copies:
        copy.start()

    width = w_query.shape[0]
    head = width // HEADS
    factor = 1.0 / math.sqrt(head)
    cols = [slice(h * head, (h + 1) * head) for h in range(HEADS)]
    heads = [slice(h * BLK, (h + 1) * BLK) for h in range(HEADS)]
    inputs = moved[0:BLK, :].astype(f32)
    scaled_one, _, normed = normalize(inputs, gain_attn[...])
    normed_b = normed.astype(b16)
    query_rows = mult(normed_b, w_query[...]).astype(b16)

    stat[...] = jnp.full_like(stat, -1e30)

    for copy in copies:
        copy.wait()

    def score(p, carry):
        key_rows = mult(feats[p], w_key[...]).astype(b16)
        allowed = seen[pl.ds(p, 1), :] > 0
        for r, c in zip(heads, cols):
            part = mult_nt(query_rows[:, c], key_rows[:, c]) * factor
            part = jnp.where(allowed, part, -1e30)
            scores[p, r, :] = part
            stat[r, :] = jnp.maximum(stat[r, :], lanes(part, jnp.maximum))
        return carry

    lax.fori_loop(0, PARTS, score, 0)
    highest = jnp.max(stat[...], axis=-1, keepdims=True)
    stat[...] = jnp.zeros_like(stat)

    def expo(p, carry):
        part = jnp.exp(scores[p] - highest)
        scores[p] = part
        stat[...] += lanes(part, jnp.add)
        return carry

    lax.fori_loop(0, PARTS, expo, 0)
    inverse_sum = 1.0 / jnp.sum(stat[...], axis=-1, keepdims=True)
    sums[...] = jnp.zeros_like(sums)

    def attend(p, carry):
        part = scores[p] * inverse_sum
        scores[p] = part
        sums[...] += mult(part.astype(b16), feats[p])
        return carry

    lax.fori_loop(0, PARTS, attend, 0)
    u_high, u_low = two_parts(sums[...])
    context = jnp.concatenate(
        [mult(u_high[r], w_value[:, c]) + mult(u_low[r], w_value[:, c]) for r, c in zip(heads, cols)],
        axis=1,
    ).astype(b16)

    core = core_ref[0]
    half = PIECES // 2

    def store(at, rows, grad):
        middle = grad.shape[0] // 2
        low, high = grad[:middle], grad[middle:]
        mine = jnp.where(core == 0, low, high)
        yours = jnp.where(core == 0, high, low).astype(b16)
        for i in range(half):
            keep[i * CHUNK + at : i * CHUNK + at + rows, :] = mine[i * rows : (i + 1) * rows]
            give[i * CHUNK + at : i * CHUNK + at + rows, :] = yours[i * rows : (i + 1) * rows]

    mixed = inputs + mult(context, w_out[...])
    scaled_two, inverse_two, normed_two = normalize(mixed, gain_mlp[...])
    normed_two_b = normed_two.astype(b16)
    activated, slope = gelu_pair(mult(normed_two_b, w_up[...]))
    activated_b = activated.astype(b16)
    output[...] = (mixed + mult(activated_b, w_down[...])).astype(b16)
    cotangent = moved[BLK : 2 * BLK, :]
    store(96, 32, mult_tn(activated_b, cotangent))
    grad_upper_b = (mult_nt(cotangent, w_down[...]) * slope).astype(b16)
    store(64, 16, mult_tn(normed_two_b, grad_upper_b[:, :width]))
    store(80, 16, mult_tn(normed_two_b, grad_upper_b[:, width:]))
    grad_normed_two = mult_nt(grad_upper_b, w_up[...])
    grad_gain_mlp = jnp.sum(grad_normed_two * scaled_two, axis=0, keepdims=True)
    grad_scaled = grad_normed_two * gain_mlp[...]
    mean_one = jnp.mean(grad_scaled, axis=-1, keepdims=True)
    mean_two = jnp.mean(grad_scaled * scaled_two, axis=-1, keepdims=True)
    grad_mixed = cotangent.astype(f32) + inverse_two * (
        grad_scaled - mean_one - scaled_two * mean_two
    )
    grad_mixed_b = grad_mixed.astype(b16)
    store(48, 16, mult_tn(context, grad_mixed_b))
    grad_context = mult_nt(grad_mixed_b, w_out[...]).astype(b16)
    store(
        32,
        16,
        jnp.concatenate(
            [
                mult_tn(u_high[r], grad_context[:, c]) + mult_tn(u_low[r], grad_context[:, c])
                for r, c in zip(heads, cols)
            ],
            axis=1,
        ),
    )
    pulled = jnp.concatenate(
        [mult_nt(grad_context[:, c], w_value[:, c]) for c in cols], axis=0
    ).astype(b16)
    stat[...] = jnp.zeros_like(stat)

    def pull(p, carry):
        part = mult_nt(pulled, feats[p])
        pulls[p] = part
        stat[...] += lanes(part * scores[p], jnp.add)
        return carry

    lax.fori_loop(0, PARTS, pull, 0)
    centre = jnp.sum(stat[...], axis=-1, keepdims=True)
    sums[...] = jnp.zeros_like(sums)

    def back(p, carry):
        part = (scores[p] * (pulls[p] - centre) * factor).astype(b16)
        sums[...] += mult(part, feats[p])
        return carry

    lax.fori_loop(0, PARTS, back, 0)
    t_high, t_low = two_parts(sums[...])
    grad_query_rows = jnp.concatenate(
        [mult(t_high[r], w_key[:, c]) + mult(t_low[r], w_key[:, c]) for r, c in zip(heads, cols)],
        axis=1,
    ).astype(b16)
    store(
        16,
        16,
        jnp.concatenate(
            [
                mult_tn(t_high[r], query_rows[:, c]) + mult_tn(t_low[r], query_rows[:, c])
                for r, c in zip(heads, cols)
            ],
            axis=1,
        ),
    )
    store(0, 16, mult_tn(normed_b, grad_query_rows))
    grad_normed = mult_nt(grad_query_rows, w_query[...])
    grad_gain_attn = jnp.sum(grad_normed * scaled_one, axis=0, keepdims=True)
    gains = jnp.concatenate([grad_gain_attn, grad_gain_mlp, jnp.zeros((6, width), f32)], axis=0)
    put_gains(give, half * CHUNK, gains)
    gains_out[...] = gains


def device_step(core_at, moved, seen, parts, weights):
    f32, b16 = jnp.float32, jnp.bfloat16
    return pl.pallas_call(
        step_kernel,
        out_shape=[
            jax.ShapeDtypeStruct((BLK, 512), b16),
            jax.ShapeDtypeStruct((2048 + TAIL, 512), b16),
            jax.ShapeDtypeStruct((2048, 512), f32),
            jax.ShapeDtypeStruct((8, 512), f32),
        ],
        in_specs=[SMEM] + [VMEM] * 10 + [pl.BlockSpec(memory_space=pl.ANY)] * PARTS,
        out_specs=[VMEM] * 4,
        scratch_shapes=[
            pltpu.VMEM((PARTS, 512, 512), b16),
            pltpu.VMEM((PARTS, 512, 512), f32),
            pltpu.VMEM((PARTS, 512, 512), f32),
            pltpu.VMEM((512, 512), f32),
            pltpu.VMEM((512, BLK), f32),
            pltpu.SemaphoreType.DMA((PARTS,)),
        ],
        compiler_params=pltpu.CompilerParams(vmem_limit_bytes=52 << 20),
        cost_estimate=pl.CostEstimate(
            flops=12 * 10**9, bytes_accessed=18 * 10**6, transcendentals=3 * 10**6
        ),
    )(core_at, moved, seen, *weights, *parts)


PIECES = 32
CHUNK = 128
TAIL = 16


def pieces_of(refs, k):
    query, key, value, out, up, down = refs
    rows = pl.ds(pl.multiple_of(k * 16, 16), 16)
    return (
        (0, query.at[rows, :]),
        (16, key.at[rows, :]),
        (32, value.at[rows, :]),
        (48, out.at[rows, :]),
        (64, up.at[rows, pl.ds(0, 512)]),
        (80, up.at[rows, pl.ds(512, 512)]),
        (96, down.at[pl.ds(pl.multiple_of(k * 32, 32), 32), :]),
    )


def put_gains(ref, at, gains):
    high = gains.astype(jnp.bfloat16)
    low = (gains - high.astype(jnp.float32)).astype(jnp.bfloat16)
    ref[at : at + TAIL, :] = jnp.concatenate([high, low], axis=0)


def take_gains(ref, at):
    tail = ref[at : at + TAIL, :].astype(jnp.float32)
    return tail[: TAIL // 2] + tail[TAIL // 2 :]


def quarters_kernel(many, index_ref, own_ref, gains_ref, *refs):
    arrived, gives, keep, gains_out = refs[:many], refs[many : many + 3], refs[many + 3], refs[many + 4]
    index = index_ref[0]
    rows = keep.shape[0]
    total = own_ref.shape[0]
    for mask in range(4):
        at = pl.ds(pl.multiple_of((index ^ mask) * rows, rows), rows)
        value = own_ref[at, :]
        for ref in arrived:
            value = value + ref[at, :].astype(jnp.float32)
        if mask:
            gives[mask - 1][0:rows, :] = value.astype(jnp.bfloat16)
        else:
            keep[...] = value
    gains = add_gains(gains_ref[...], [take_gains(ref, total) for ref in arrived])
    for give in gives:
        put_gains(give, rows, gains)
    gains_out[...] = gains


def add_gains(own, arrived):
    high = own.astype(jnp.bfloat16).astype(jnp.float32)
    own = high + (own - high).astype(jnp.bfloat16).astype(jnp.float32)
    if len(arrived) == 1:
        return own + arrived[0]
    return (own + arrived[0]) + (arrived[1] + arrived[2])


def chunk_kernel(own_ref, gains_ref, *refs):
    arrived, give = refs[:3], refs[3]
    rows = own_ref.shape[0]
    value = own_ref[...]
    for ref in arrived:
        value = value + ref[0:rows, :].astype(jnp.float32)
    give[0:rows, :] = value.astype(jnp.bfloat16)
    put_gains(give, rows, add_gains(gains_ref[...], [take_gains(ref, rows) for ref in arrived]))


def last_kernel(own_ref, *refs):
    arrived, chunk, gains = refs[:3], refs[3], refs[4]
    rows = chunk.shape[0]
    a, b, c, d = (ref[0:rows, :].astype(jnp.float32) for ref in (own_ref, *arrived))
    chunk[...] = ((a + b) + (c + d)).astype(jnp.bfloat16)
    a, b, c, d = (take_gains(ref, rows) for ref in (own_ref, *arrived))
    put_gains(gains, 0, (a + b) + (c + d))


def place_kernel(where_ref, *refs):
    own, other, gains_own, gains_other = refs[0:4], refs[4:8], refs[8], refs[9]
    grads, gains_out = refs[10:16], refs[16]
    core, y, z = where_ref[0], where_ref[1], where_ref[2]
    for side, group in enumerate((own, other)):
        holder = core ^ side
        one = jnp.where(holder == 0, y, z)
        two = jnp.where(holder == 0, z, y)
        for m1 in range(4):
            for m2 in range(4):
                k = holder * 16 + (one ^ m1) * 4 + (two ^ m2)
                for at, piece in pieces_of(grads, k):
                    piece[...] = group[m1][m2 * CHUNK + at : m2 * CHUNK + at + piece.shape[0], :]
    gains = jnp.where(core == 0, take_gains(gains_own, 0), take_gains(gains_other, 0))
    gains_out[...] = gains.astype(jnp.bfloat16)


def call(kernel, outs, *operands, scalars=0):
    return pl.pallas_call(
        kernel,
        out_shape=[jax.ShapeDtypeStruct(shape, dtype) for shape, dtype in outs],
        in_specs=[SMEM] * scalars + [VMEM] * (len(operands) - scalars),
        out_specs=[VMEM] * len(outs),
        compiler_params=pltpu.CompilerParams(vmem_limit_bytes=48 << 20),
    )(*operands)


def sum_everywhere(output, give, keep, gains):
    core, y, z = (lax.axis_index(name) for name in ("core", "y", "z"))
    one_at = jnp.where(core == 0, y, z).astype(jnp.int32).reshape(1)
    two_at = jnp.where(core == 0, z, y).astype(jnp.int32).reshape(1)
    b16, f32 = jnp.bfloat16, jnp.float32

    arrived = [send(give, CORE)]
    for rows, index, route, count in ((512, one_at, first, 1), (128, two_at, second, 3)):
        *gives, keep, gains = call(
            lambda *refs, count=count: quarters_kernel(count, *refs),
            [((rows + TAIL, 512), b16)] * 3 + [((rows, 512), f32), ((8, 512), f32)],
            index, keep, gains, *arrived, scalars=1,
        )
        arrived = [send(give, route(mask)) for mask, give in enumerate(gives, 1)]
    output, *arrived = lax.optimization_barrier((send(output, SWAP), *arrived))
    (give,) = call(chunk_kernel, [((128 + TAIL, 512), b16)], keep, gains, *arrived)
    arrived = [send(give, along_x(mask)) for mask in (1, 2, 3)]
    chunk, gains = call(last_kernel, [((128, 512), b16), ((TAIL, 512), b16)], give, *arrived)

    mine = jnp.concatenate([chunk] + [send(chunk, second(mask)) for mask in (1, 2, 3)])
    own = [mine] + [send(mine, first(mask)) for mask in (1, 2, 3)]
    other = [send(part, CORE) for part in own]
    gains_other = send(gains, CORE)
    where = jnp.stack([core, y, z]).astype(jnp.int32)
    *weights, gains = call(
        place_kernel,
        [((512, 512), b16)] * 4 + [((512, 1024), b16), ((1024, 512), b16), ((8, 512), b16)],
        where, *own, *other, gains, gains_other, scalars=1,
    )
    return (output[None], *weights, gains[0], gains[1])


def gather_features(own, others):
    own = send(own, SWAP)
    mine = jnp.concatenate([own] + [send(own, first(mask)) for mask in (1, 2, 3)])
    mine, others = lax.optimization_barrier((mine, others))
    group = [mine] + [send(mine, second(mask)) for mask in (1, 2, 3)]
    parts = group + [send(part, CORE) for part in group]
    core, y, z = (lax.axis_index(name) for name in ("core", "y", "z"))
    side, two, one = (jnp.asarray(i) for i in np.unravel_index(np.arange(32), (2, 4, 4)))
    holder = core ^ side
    block_y = jnp.where(holder == 0, y ^ one, y ^ two)
    block_z = jnp.where(holder == 0, z ^ two, z ^ one)
    return parts, block_z * 8 + holder * 4 + block_y, send(others, SWAP)


def local(
    queries,
    features,
    visible,
    cotangent,
    w_query,
    w_key,
    w_value,
    w_out,
    w_up,
    w_down,
    gain_attn,
    gain_mlp,
):
    seen = jnp.pad(visible[0].astype(jnp.bfloat16), ((0, 15), (0, 512 - visible.shape[-1])))
    parts, blocks, moved = gather_features(
        features[0], jnp.concatenate([queries[0], cotangent[0], seen])
    )
    seen = jnp.take(moved[2 * BLK].astype(jnp.float32), blocks)
    core_at = lax.axis_index("core").astype(jnp.int32).reshape(1)
    return sum_everywhere(
        *device_step(
            core_at,
            moved,
            jnp.repeat(seen, BLK).reshape(PARTS, 512),
            parts,
            (w_query, w_key, w_value, w_out, w_up, w_down, gain_attn[None], gain_mlp[None]),
        )
    )


def solution(mesh):
    parts = Mesh(mesh.devices.reshape(SIZES), AXES)
    split = P(ROOM, GEOM, None)
    return jax.shard_map(
        local,
        mesh=parts,
        in_specs=(split,) * 4 + (P(),) * 8,
        out_specs=(split,) + (P(),) * 8,
        check_vma=False,
    )
```

```python
import math

import jax
import jax.numpy as jnp
import numpy as np
from jax import lax
from jax.experimental import pallas as pl
from jax.experimental.pallas import tpu as pltpu
from jax.sharding import Mesh, PartitionSpec as P

HEADS = 4
BLK = 128
EPSILON = 1e-05
GELU_COEF = math.sqrt(2.0 / math.pi)

AXES = ("x_hi", "core", "z", "x_lo", "y")
SIZES = (2, 2, 4, 2, 4)
ROOM = ("x_hi", "core")
GEOM = ("z", "x_lo", "y")
VMEM = pl.BlockSpec(memory_space=pltpu.VMEM)
SMEM = pl.BlockSpec(memory_space=pltpu.SMEM)


def pairs_of(move):
    pairs = []
    for source in range(math.prod(SIZES)):
        target = move(*(int(i) for i in np.unravel_index(source, SIZES)))
        pairs.append((source, int(np.ravel_multi_index(target, SIZES))))
    return pairs


SWAP = pairs_of(lambda xh, c, z, xl, y: (xh, xl, z, c, y))
CORE = pairs_of(lambda xh, c, z, xl, y: (xh, 1 - c, z, xl, y))


def first(mask):
    return pairs_of(
        lambda xh, c, z, xl, y: (xh, c, z, xl, y ^ mask) if c == 0 else (xh, c, z ^ mask, xl, y)
    )


def first_swapped(mask):
    after = dict(first(mask))
    return [(source, after[target]) for source, target in SWAP]


def second(mask):
    return pairs_of(
        lambda xh, c, z, xl, y: (xh, c, z ^ mask, xl, y) if c == 0 else (xh, c, z, xl, y ^ mask)
    )


def along_x(mask):
    return pairs_of(lambda xh, c, z, xl, y: (xh ^ (mask >> 1), c, z, xl ^ (mask & 1), y))


def send(value, pairs):
    return lax.ppermute(value, AXES, pairs)


def normalize(inputs, gain):
    center = inputs - jnp.mean(inputs, axis=-1, keepdims=True)
    inverse = lax.rsqrt(jnp.mean(center * center, axis=-1, keepdims=True) + EPSILON)
    scaled = center * inverse
    return (scaled, inverse, scaled * gain)


def gelu_pair(inputs):
    inner = GELU_COEF * (inputs + 0.044715 * inputs * inputs * inputs)
    tangent = jnp.tanh(inner)
    value = 0.5 * inputs * (1.0 + tangent)
    slope = 0.5 * (1.0 + tangent) + 0.5 * inputs * (1.0 - tangent * tangent) * GELU_COEF * (
        1.0 + 3.0 * 0.044715 * inputs * inputs
    )
    return (value, slope)


def mult(left, right):
    return jnp.dot(left, right, preferred_element_type=jnp.float32)


def mult_nt(left, right):
    return lax.dot_general(
        left, right, (((1,), (1,)), ((), ())), preferred_element_type=jnp.float32
    )


def mult_tn(left, right):
    return lax.dot_general(
        left, right, (((0,), (0,)), ((), ())), preferred_element_type=jnp.float32
    )


def two_parts(value):
    high = value.astype(jnp.bfloat16)
    low = (value - high.astype(jnp.float32)).astype(jnp.bfloat16)
    return high, low


PARTS = 8
def lanes(value, combine):
    out = value[:, 0:BLK]
    for at in range(BLK, value.shape[1], BLK):
        out = combine(out, value[:, at : at + BLK])
    return out


def step_kernel(core_ref, moved, seen, w_query, w_key, w_value, w_out, w_up, w_down, gain_attn, gain_mlp, *refs):
    parts, (output, give, keep, gains_out) = refs[:PARTS], refs[PARTS : PARTS + 4]
    feats, scores, pulls, sums, stat, sems = refs[PARTS + 4 :]
    f32, b16 = jnp.float32, jnp.bfloat16
    copies = [pltpu.make_async_copy(parts[p], feats.at[p], sems.at[p]) for p in range(PARTS)]
    for copy in copies:
        copy.start()

    width = w_query.shape[0]
    head = width // HEADS
    factor = 1.0 / math.sqrt(head)
    cols = [slice(h * head, (h + 1) * head) for h in range(HEADS)]
    heads = [slice(h * BLK, (h + 1) * BLK) for h in range(HEADS)]
    inputs = moved[0:BLK, :].astype(f32)
    scaled_one, _, normed = normalize(inputs, gain_attn[...])
    normed_b = normed.astype(b16)
    query_rows = mult(normed_b, w_query[...]).astype(b16)

    blank = jnp.zeros((BLK, head), b16)
    query_pairs = jnp.concatenate(
        [
            jnp.concatenate(
                [query_rows[:, c] if h % 2 == side else blank for side in range(2)], axis=1
            )
            for h, c in enumerate(cols)
        ],
        axis=0,
    )
    pair_rows = [slice(0, 2 * BLK), slice(2 * BLK, 4 * BLK)]
    pair_cols = [slice(0, 2 * head), slice(2 * head, 4 * head)]

    stat[...] = jnp.full_like(stat, -1e30)

    for p in range(PARTS):
        copies[p].wait()
        key_rows = mult(feats[p], w_key[...]).astype(b16)
        allowed = seen[p : p + 1, :] > 0
        for r, c in zip(pair_rows, pair_cols):
            part = mult_nt(query_pairs[r, :], key_rows[:, c]) * factor
            part = jnp.where(allowed, part, -1e30)
            scores[p, r, :] = part
            stat[r, :] = jnp.maximum(stat[r, :], lanes(part, jnp.maximum))

    highest = jnp.max(stat[...], axis=-1, keepdims=True)
    stat[...] = jnp.zeros_like(stat)

    for p in range(PARTS):
        part = jnp.exp(scores[p] - highest)
        scores[p] = part
        stat[...] += lanes(part, jnp.add)

    inverse_sum = 1.0 / jnp.sum(stat[...], axis=-1, keepdims=True)
    sums[...] = jnp.zeros_like(sums)

    for p in range(PARTS):
        part = scores[p] * inverse_sum
        scores[p] = part
        sums[...] += mult(part.astype(b16), feats[p])

    u_high, u_low = two_parts(sums[...])
    context = jnp.concatenate(
        [mult(u_high[r], w_value[:, c]) + mult(u_low[r], w_value[:, c]) for r, c in zip(heads, cols)],
        axis=1,
    ).astype(b16)

    core = core_ref[0]
    half = PIECES // 2

    def store(at, rows, grad):
        middle = grad.shape[0] // 2
        low, high = grad[:middle], grad[middle:]
        mine = jnp.where(core == 0, low, high).astype(b16)
        yours = jnp.where(core == 0, high, low).astype(b16)
        for i in range(half):
            keep[i * CHUNK + at : i * CHUNK + at + rows, :] = mine[i * rows : (i + 1) * rows]
            give[i * CHUNK + at : i * CHUNK + at + rows, :] = yours[i * rows : (i + 1) * rows]

    mixed = inputs + mult(context, w_out[...])
    scaled_two, inverse_two, normed_two = normalize(mixed, gain_mlp[...])
    normed_two_b = normed_two.astype(b16)
    activated, slope = gelu_pair(mult(normed_two_b, w_up[...]))
    activated_b = activated.astype(b16)
    output[...] = (mixed + mult(activated_b, w_down[...])).astype(b16)
    cotangent = moved[BLK : 2 * BLK, :]
    store(96, 32, mult_tn(activated_b, cotangent))
    grad_upper_b = (mult_nt(cotangent, w_down[...]) * slope).astype(b16)
    store(64, 16, mult_tn(normed_two_b, grad_upper_b[:, :width]))
    store(80, 16, mult_tn(normed_two_b, grad_upper_b[:, width:]))
    grad_normed_two = mult_nt(grad_upper_b, w_up[...])
    grad_gain_mlp = jnp.sum(grad_normed_two * scaled_two, axis=0, keepdims=True)
    grad_scaled = grad_normed_two * gain_mlp[...]
    mean_one = jnp.mean(grad_scaled, axis=-1, keepdims=True)
    mean_two = jnp.mean(grad_scaled * scaled_two, axis=-1, keepdims=True)
    grad_mixed = cotangent.astype(f32) + inverse_two * (
        grad_scaled - mean_one - scaled_two * mean_two
    )
    grad_mixed_b = grad_mixed.astype(b16)
    store(48, 16, mult_tn(context, grad_mixed_b))
    grad_context = mult_nt(grad_mixed_b, w_out[...]).astype(b16)
    store(
        32,
        16,
        jnp.concatenate(
            [
                mult_tn(u_high[r], grad_context[:, c]) + mult_tn(u_low[r], grad_context[:, c])
                for r, c in zip(heads, cols)
            ],
            axis=1,
        ),
    )
    pulled = jnp.concatenate(
        [mult_nt(grad_context[:, c], w_value[:, c]) for c in cols], axis=0
    ).astype(b16)
    stat[...] = jnp.zeros_like(stat)

    for p in range(PARTS):
        part = mult_nt(pulled, feats[p])
        pulls[p] = part
        stat[...] += lanes(part * scores[p], jnp.add)

    centre = jnp.sum(stat[...], axis=-1, keepdims=True)
    sums[...] = jnp.zeros_like(sums)

    for p in range(PARTS):
        part = (scores[p] * (pulls[p] - centre) * factor).astype(b16)
        sums[...] += mult(part, feats[p])

    t_high, t_low = two_parts(sums[...])
    grad_query_rows = jnp.concatenate(
        [mult(t_high[r], w_key[:, c]) + mult(t_low[r], w_key[:, c]) for r, c in zip(heads, cols)],
        axis=1,
    ).astype(b16)
    store(
        16,
        16,
        jnp.concatenate(
            [
                mult_tn(t_high[r], query_rows[:, c]) + mult_tn(t_low[r], query_rows[:, c])
                for r, c in zip(heads, cols)
            ],
            axis=1,
        ),
    )
    store(0, 16, mult_tn(normed_b, grad_query_rows))
    grad_normed = mult_nt(grad_query_rows, w_query[...])
    grad_gain_attn = jnp.sum(grad_normed * scaled_one, axis=0, keepdims=True)
    gains = jnp.concatenate([grad_gain_attn, grad_gain_mlp, jnp.zeros((6, width), f32)], axis=0)
    put_gains(give, half * CHUNK, gains)
    gains_out[...] = gains


def device_step(core_at, moved, seen, parts, weights):
    f32, b16 = jnp.float32, jnp.bfloat16
    return pl.pallas_call(
        step_kernel,
        out_shape=[
            jax.ShapeDtypeStruct((BLK, 512), b16),
            jax.ShapeDtypeStruct((2048 + TAIL, 512), b16),
            jax.ShapeDtypeStruct((2048, 512), b16),
            jax.ShapeDtypeStruct((8, 512), f32),
        ],
        in_specs=[SMEM] + [VMEM] * 10 + [pl.BlockSpec(memory_space=pl.ANY)] * PARTS,
        out_specs=[VMEM] * 4,
        scratch_shapes=[
            pltpu.VMEM((PARTS, 512, 512), b16),
            pltpu.VMEM((PARTS, 512, 512), f32),
            pltpu.VMEM((PARTS, 512, 512), f32),
            pltpu.VMEM((512, 512), f32),
            pltpu.VMEM((512, BLK), f32),
            pltpu.SemaphoreType.DMA((PARTS,)),
        ],
        compiler_params=pltpu.CompilerParams(vmem_limit_bytes=52 << 20),
        cost_estimate=pl.CostEstimate(
            flops=12 * 10**9, bytes_accessed=18 * 10**6, transcendentals=3 * 10**6
        ),
    )(core_at, moved, seen, *weights, *parts)


PIECES = 32
CHUNK = 128
TAIL = 16


def pieces_of(refs, k):
    query, key, value, out, up, down = refs
    rows = pl.ds(pl.multiple_of(k * 16, 16), 16)
    return (
        (0, query.at[rows, :]),
        (16, key.at[rows, :]),
        (32, value.at[rows, :]),
        (48, out.at[rows, :]),
        (64, up.at[rows, pl.ds(0, 512)]),
        (80, up.at[rows, pl.ds(512, 512)]),
        (96, down.at[pl.ds(pl.multiple_of(k * 32, 32), 32), :]),
    )


def put_gains(ref, at, gains):
    high = gains.astype(jnp.bfloat16)
    low = (gains - high.astype(jnp.float32)).astype(jnp.bfloat16)
    ref[at : at + TAIL, :] = jnp.concatenate([high, low], axis=0)


def take_gains(ref, at):
    tail = ref[at : at + TAIL, :].astype(jnp.float32)
    return tail[: TAIL // 2] + tail[TAIL // 2 :]


def quarters_kernel(many, index_ref, own_ref, gains_ref, *refs):
    arrived, gives, keep, gains_out = refs[:many], refs[many : many + 3], refs[many + 3], refs[many + 4]
    index = index_ref[0]
    rows = keep.shape[0]
    total = own_ref.shape[0]
    for mask in range(4):
        at = pl.ds(pl.multiple_of((index ^ mask) * rows, rows), rows)
        value = own_ref[at, :].astype(jnp.float32)
        for ref in arrived:
            value = value + ref[at, :].astype(jnp.float32)
        if mask:
            gives[mask - 1][0:rows, :] = value.astype(jnp.bfloat16)
        else:
            keep[...] = value
    gains = add_gains(gains_ref[...], [take_gains(ref, total) for ref in arrived])
    for give in gives:
        put_gains(give, rows, gains)
    gains_out[...] = gains


def add_gains(own, arrived):
    high = own.astype(jnp.bfloat16).astype(jnp.float32)
    own = high + (own - high).astype(jnp.bfloat16).astype(jnp.float32)
    if len(arrived) == 1:
        return own + arrived[0]
    return (own + arrived[0]) + (arrived[1] + arrived[2])


def chunk_kernel(own_ref, gains_ref, *refs):
    arrived, give = refs[:3], refs[3]
    rows = own_ref.shape[0]
    value = own_ref[...]
    for ref in arrived:
        value = value + ref[0:rows, :].astype(jnp.float32)
    give[0:rows, :] = value.astype(jnp.bfloat16)
    put_gains(give, rows, add_gains(gains_ref[...], [take_gains(ref, rows) for ref in arrived]))


def last_kernel(own_ref, *refs):
    arrived, chunk, gains = refs[:3], refs[3], refs[4]
    rows = chunk.shape[0]
    a, b, c, d = (ref[0:rows, :].astype(jnp.float32) for ref in (own_ref, *arrived))
    chunk[...] = ((a + b) + (c + d)).astype(jnp.bfloat16)
    a, b, c, d = (take_gains(ref, rows) for ref in (own_ref, *arrived))
    put_gains(gains, 0, (a + b) + (c + d))


def place_kernel(where_ref, *refs):
    own, other, gains_own = refs[0:4], refs[4:8], refs[8]
    grads, gain_attn, gain_mlp = refs[9:15], refs[15], refs[16]
    core, y, z = where_ref[0], where_ref[1], where_ref[2]
    for side, group in enumerate((own, other)):
        holder = core ^ side
        one = jnp.where(holder == 0, y, z)
        two = jnp.where(holder == 0, z, y)
        for m1 in range(4):
            for m2 in range(4):
                k = holder * 16 + (one ^ m1) * 4 + (two ^ m2)
                for at, piece in pieces_of(grads, k):
                    piece[...] = group[m1][m2 * CHUNK + at : m2 * CHUNK + at + piece.shape[0], :]
    gains = jnp.where(core == 0, take_gains(gains_own, 0), take_gains(other[0], 4 * CHUNK))
    gain_attn[...] = gains[0].astype(jnp.bfloat16)
    gain_mlp[...] = gains[1].astype(jnp.bfloat16)


def call(kernel, outs, *operands, scalars=0):
    return pl.pallas_call(
        kernel,
        out_shape=[jax.ShapeDtypeStruct(shape, dtype) for shape, dtype in outs],
        in_specs=[SMEM] * scalars + [VMEM] * (len(operands) - scalars),
        out_specs=[VMEM] * len(outs),
        compiler_params=pltpu.CompilerParams(vmem_limit_bytes=48 << 20),
    )(*operands)


def sum_everywhere(output, give, keep, gains):
    core, y, z = (lax.axis_index(name) for name in ("core", "y", "z"))
    one_at = jnp.where(core == 0, y, z).astype(jnp.int32).reshape(1)
    two_at = jnp.where(core == 0, z, y).astype(jnp.int32).reshape(1)
    b16, f32 = jnp.bfloat16, jnp.float32

    arrived = [send(give, CORE)]
    for rows, index, route, count in ((512, one_at, first, 1), (128, two_at, second, 3)):
        *gives, keep, gains = call(
            lambda *refs, count=count: quarters_kernel(count, *refs),
            [((rows + TAIL, 512), b16)] * 3 + [((rows, 512), f32), ((8, 512), f32)],
            index, keep, gains, *arrived, scalars=1,
        )
        arrived = [send(give, route(mask)) for mask, give in enumerate(gives, 1)]
        if count == 1:
            output, *arrived = lax.optimization_barrier((send(output, SWAP), *arrived))
    (give,) = call(chunk_kernel, [((128 + TAIL, 512), b16)], keep, gains, *arrived)
    arrived = [send(give, along_x(mask)) for mask in (1, 2, 3)]
    chunk, gains = call(last_kernel, [((128, 512), b16), ((TAIL, 512), b16)], give, *arrived)

    mine = jnp.concatenate([chunk] + [send(chunk, second(mask)) for mask in (1, 2, 3)])
    own = [mine] + [send(mine, first(mask)) for mask in (1, 2, 3)]
    other = [send(jnp.concatenate([mine, gains]), CORE)] + [send(part, CORE) for part in own[1:]]
    where = jnp.stack([core, y, z]).astype(jnp.int32)
    placed = call(
        place_kernel,
        [((512, 512), b16)] * 4 + [((512, 1024), b16), ((1024, 512), b16)] + [((512,), b16)] * 2,
        where, *own, *other, gains, scalars=1,
    )
    return (output[None], *placed)


def gather_features(own, others):
    mine = jnp.concatenate([send(own, first_swapped(mask)) for mask in range(4)])
    mine, others = lax.optimization_barrier((mine, others))
    group = [mine] + [send(mine, second(mask)) for mask in (1, 2, 3)]
    parts = group + [send(part, CORE) for part in group]
    core, y, z = (lax.axis_index(name) for name in ("core", "y", "z"))
    side, two, one = (jnp.asarray(i) for i in np.unravel_index(np.arange(32), (2, 4, 4)))
    holder = core ^ side
    block_y = jnp.where(holder == 0, y ^ one, y ^ two)
    block_z = jnp.where(holder == 0, z ^ two, z ^ one)
    return parts, block_z * 8 + holder * 4 + block_y, send(others, SWAP)


def local(
    queries,
    features,
    visible,
    cotangent,
    w_query,
    w_key,
    w_value,
    w_out,
    w_up,
    w_down,
    gain_attn,
    gain_mlp,
):
    seen = jnp.pad(visible[0].astype(jnp.bfloat16), ((0, 15), (0, 512 - visible.shape[-1])))
    parts, blocks, moved = gather_features(
        features[0], jnp.concatenate([queries[0], cotangent[0], seen])
    )
    seen = jnp.take(moved[2 * BLK].astype(jnp.float32), blocks)
    core_at = lax.axis_index("core").astype(jnp.int32).reshape(1)
    return sum_everywhere(
        *device_step(
            core_at,
            moved,
            jnp.repeat(seen, BLK).reshape(PARTS, 512),
            parts,
            (w_query, w_key, w_value, w_out, w_up, w_down, gain_attn[None], gain_mlp[None]),
        )
    )


def solution(mesh):
    parts = Mesh(mesh.devices.reshape(SIZES), AXES)
    split = P(ROOM, GEOM, None)
    return jax.shard_map(
        local,
        mesh=parts,
        in_specs=(split,) * 4 + (P(),) * 8,
        out_specs=(split,) + (P(),) * 8,
        check_vma=False,
    )
```

```python
import math

import jax
import jax.numpy as jnp
import numpy as np
from jax import lax
from jax.experimental import pallas as pl
from jax.experimental.pallas import tpu as pltpu
from jax.sharding import Mesh, PartitionSpec as P

HEADS = 4
BLK = 128
EPSILON = 1e-05
GELU_COEF = math.sqrt(2.0 / math.pi)

AXES = ("x_hi", "core", "z", "x_lo", "y")
SIZES = (2, 2, 4, 2, 4)
ROOM = ("x_hi", "core")
GEOM = ("z", "x_lo", "y")
VMEM = pl.BlockSpec(memory_space=pltpu.VMEM)
SMEM = pl.BlockSpec(memory_space=pltpu.SMEM)
ANY = pl.BlockSpec(memory_space=pl.ANY)
FAR = 2
ORDER = (2, 1, 3)


def pairs_of(move):
    pairs = []
    for source in range(math.prod(SIZES)):
        target = move(*(int(i) for i in np.unravel_index(source, SIZES)))
        pairs.append((source, int(np.ravel_multi_index(target, SIZES))))
    return pairs


SWAP = pairs_of(lambda xh, c, z, xl, y: (xh, xl, z, c, y))
CORE = pairs_of(lambda xh, c, z, xl, y: (xh, 1 - c, z, xl, y))


def first(mask):
    return pairs_of(
        lambda xh, c, z, xl, y: (xh, c, z, xl, y ^ mask) if c == 0 else (xh, c, z ^ mask, xl, y)
    )


def first_swapped(mask):
    after = dict(first(mask))
    return [(source, after[target]) for source, target in SWAP]


def second(mask):
    return pairs_of(
        lambda xh, c, z, xl, y: (xh, c, z ^ mask, xl, y) if c == 0 else (xh, c, z, xl, y ^ mask)
    )


def along_x(mask):
    return pairs_of(lambda xh, c, z, xl, y: (xh ^ (mask >> 1), c, z, xl ^ (mask & 1), y))


def send(value, pairs):
    return lax.ppermute(value, AXES, pairs)


def normalize(inputs, gain):
    center = inputs - jnp.mean(inputs, axis=-1, keepdims=True)
    inverse = lax.rsqrt(jnp.mean(center * center, axis=-1, keepdims=True) + EPSILON)
    scaled = center * inverse
    return (scaled, inverse, scaled * gain)


def gelu_pair(inputs):
    inner = GELU_COEF * (inputs + 0.044715 * inputs * inputs * inputs)
    tangent = jnp.tanh(inner)
    value = 0.5 * inputs * (1.0 + tangent)
    slope = 0.5 * (1.0 + tangent) + 0.5 * inputs * (1.0 - tangent * tangent) * GELU_COEF * (
        1.0 + 3.0 * 0.044715 * inputs * inputs
    )
    return (value, slope)


def mult(left, right):
    return jnp.dot(left, right, preferred_element_type=jnp.float32)


def mult_nt(left, right):
    return lax.dot_general(
        left, right, (((1,), (1,)), ((), ())), preferred_element_type=jnp.float32
    )


def mult_tn(left, right):
    return lax.dot_general(
        left, right, (((0,), (0,)), ((), ())), preferred_element_type=jnp.float32
    )


def two_parts(value):
    high = value.astype(jnp.bfloat16)
    low = (value - high.astype(jnp.float32)).astype(jnp.bfloat16)
    return high, low


PARTS = 8
PIECES = 32
CHUNK = 128
TAIL = 16
LAYOUT = ((0, 16), (16, 16), (32, 16), (48, 16), (64, 16), (80, 16), (96, 32))


def lanes(value, combine):
    out = value[:, 0:BLK]
    for at in range(BLK, value.shape[1], BLK):
        out = combine(out, value[:, at : at + BLK])
    return out


def step_kernel(where, moved, seen, w_query, w_key, w_value, w_out, w_up, w_down, gain_attn, gain_mlp, *refs):
    parts, (output, gains_out), refs = refs[:PARTS], refs[PARTS : PARTS + 2], refs[PARTS + 2 :]
    gives, keeps, refs = refs[:4], refs[4:8], refs[8:]
    feats, scores, pulls, sums, stat, give, keep, tail, sems, out_sems = refs
    f32, b16 = jnp.float32, jnp.bfloat16
    copies = [pltpu.make_async_copy(parts[p], feats.at[p], sems.at[p]) for p in range(PARTS)]
    for copy in copies:
        copy.start()

    width = w_query.shape[0]
    head = width // HEADS
    factor = 1.0 / math.sqrt(head)
    cols = [slice(h * head, (h + 1) * head) for h in range(HEADS)]
    heads = [slice(h * BLK, (h + 1) * BLK) for h in range(HEADS)]
    inputs = moved[0:BLK, :].astype(f32)
    scaled_one, _, normed = normalize(inputs, gain_attn[...])
    normed_b = normed.astype(b16)
    query_rows = mult(normed_b, w_query[...]).astype(b16)

    blank = jnp.zeros((BLK, head), b16)
    query_pairs = jnp.concatenate(
        [
            jnp.concatenate(
                [query_rows[:, c] if h % 2 == side else blank for side in range(2)], axis=1
            )
            for h, c in enumerate(cols)
        ],
        axis=0,
    )
    pair_rows = [slice(0, 2 * BLK), slice(2 * BLK, 4 * BLK)]
    pair_cols = [slice(0, 2 * head), slice(2 * head, 4 * head)]

    stat[...] = jnp.full_like(stat, -1e30)

    for p in range(PARTS):
        copies[p].wait()
        key_rows = mult(feats[p], w_key[...]).astype(b16)
        allowed = seen[p : p + 1, :] > 0
        for r, c in zip(pair_rows, pair_cols):
            part = mult_nt(query_pairs[r, :], key_rows[:, c]) * factor
            part = jnp.where(allowed, part, -1e30)
            scores[p, r, :] = part
            stat[r, :] = jnp.maximum(stat[r, :], lanes(part, jnp.maximum))

    highest = jnp.max(stat[...], axis=-1, keepdims=True)
    stat[...] = jnp.zeros_like(stat)

    for p in range(PARTS):
        part = jnp.exp(scores[p] - highest)
        scores[p] = part
        stat[...] += lanes(part, jnp.add)

    inverse_sum = 1.0 / jnp.sum(stat[...], axis=-1, keepdims=True)
    sums[...] = jnp.zeros_like(sums)

    for p in range(PARTS):
        part = scores[p] * inverse_sum
        scores[p] = part
        sums[...] += mult(part.astype(b16), feats[p])

    u_high, u_low = two_parts(sums[...])
    context = jnp.concatenate(
        [mult(u_high[r], w_value[:, c]) + mult(u_low[r], w_value[:, c]) for r, c in zip(heads, cols)],
        axis=1,
    ).astype(b16)

    core = where[0]
    half = PIECES // 2

    def store(at, rows, grad):
        middle = grad.shape[0] // 2
        low, high = grad[:middle], grad[middle:]
        mine = jnp.where(core == 0, low, high).astype(b16)
        yours = jnp.where(core == 0, high, low).astype(b16)
        for i in range(half):
            row = i % 4 * CHUNK + at
            keep[i // 4, row : row + rows, :] = mine[i * rows : (i + 1) * rows]
            give[i // 4, row : row + rows, :] = yours[i * rows : (i + 1) * rows]

    mixed = inputs + mult(context, w_out[...])
    scaled_two, inverse_two, normed_two = normalize(mixed, gain_mlp[...])
    normed_two_b = normed_two.astype(b16)
    activated, slope = gelu_pair(mult(normed_two_b, w_up[...]))
    activated_b = activated.astype(b16)
    output[...] = (mixed + mult(activated_b, w_down[...])).astype(b16)
    cotangent = moved[BLK : 2 * BLK, :]
    store(96, 32, mult_tn(activated_b, cotangent))
    grad_upper_b = (mult_nt(cotangent, w_down[...]) * slope).astype(b16)
    store(64, 16, mult_tn(normed_two_b, grad_upper_b[:, :width]))
    store(80, 16, mult_tn(normed_two_b, grad_upper_b[:, width:]))
    grad_normed_two = mult_nt(grad_upper_b, w_up[...])
    grad_gain_mlp = jnp.sum(grad_normed_two * scaled_two, axis=0, keepdims=True)
    grad_scaled = grad_normed_two * gain_mlp[...]
    mean_one = jnp.mean(grad_scaled, axis=-1, keepdims=True)
    mean_two = jnp.mean(grad_scaled * scaled_two, axis=-1, keepdims=True)
    grad_mixed = cotangent.astype(f32) + inverse_two * (
        grad_scaled - mean_one - scaled_two * mean_two
    )
    grad_mixed_b = grad_mixed.astype(b16)
    store(48, 16, mult_tn(context, grad_mixed_b))
    grad_context = mult_nt(grad_mixed_b, w_out[...]).astype(b16)
    store(
        32,
        16,
        jnp.concatenate(
            [
                mult_tn(u_high[r], grad_context[:, c]) + mult_tn(u_low[r], grad_context[:, c])
                for r, c in zip(heads, cols)
            ],
            axis=1,
        ),
    )
    pulled = jnp.concatenate(
        [mult_nt(grad_context[:, c], w_value[:, c]) for c in cols], axis=0
    ).astype(b16)
    stat[...] = jnp.zeros_like(stat)

    for p in range(PARTS):
        part = mult_nt(pulled, feats[p])
        pulls[p] = part
        stat[...] += lanes(part * scores[p], jnp.add)

    centre = jnp.sum(stat[...], axis=-1, keepdims=True)
    sums[...] = jnp.zeros_like(sums)

    for p in range(PARTS):
        part = (scores[p] * (pulls[p] - centre) * factor).astype(b16)
        sums[...] += mult(part, feats[p])

    t_high, t_low = two_parts(sums[...])
    grad_query_rows = jnp.concatenate(
        [mult(t_high[r], w_key[:, c]) + mult(t_low[r], w_key[:, c]) for r, c in zip(heads, cols)],
        axis=1,
    ).astype(b16)
    store(
        16,
        16,
        jnp.concatenate(
            [
                mult_tn(t_high[r], query_rows[:, c]) + mult_tn(t_low[r], query_rows[:, c])
                for r, c in zip(heads, cols)
            ],
            axis=1,
        ),
    )
    store(0, 16, mult_tn(normed_b, grad_query_rows))
    grad_normed = mult_nt(grad_query_rows, w_query[...])
    grad_gain_attn = jnp.sum(grad_normed * scaled_one, axis=0, keepdims=True)
    gains = jnp.concatenate([grad_gain_attn, grad_gain_mlp, jnp.zeros((6, width), f32)], axis=0)
    put_gains(tail, 0, gains)
    gains_out[...] = gains
    one, two = where[1], where[2]
    copies = [
        pltpu.make_async_copy(tail, gives[FAR].at[pl.ds(4 * CHUNK, TAIL)], out_sems.at[8])
    ]
    for i, mask in enumerate(ORDER + (0,)):
        for j, (held, outs, index) in enumerate(((give, gives, two), (keep, keeps, one))):
            copies.append(
                pltpu.make_async_copy(
                    held.at[index ^ mask],
                    outs[mask].at[pl.ds(0, 4 * CHUNK)],
                    out_sems.at[2 * i + j],
                )
            )
    for copy in copies:
        copy.start()
    for copy in copies:
        copy.wait()


def device_step(where, moved, seen, parts, weights):
    f32, b16 = jnp.float32, jnp.bfloat16
    quarters = [(4 * CHUNK + (TAIL if mask == FAR else 0), 512) for mask in range(4)]
    return pl.pallas_call(
        step_kernel,
        out_shape=[
            jax.ShapeDtypeStruct((BLK, 512), b16),
            jax.ShapeDtypeStruct((8, 512), f32),
        ]
        + [jax.ShapeDtypeStruct(shape, b16) for shape in quarters]
        + [jax.ShapeDtypeStruct((4 * CHUNK, 512), b16)] * 4,
        in_specs=[SMEM] + [VMEM] * 10 + [ANY] * PARTS,
        out_specs=[VMEM] * 2 + [ANY] * 8,
        scratch_shapes=[
            pltpu.VMEM((PARTS, 512, 512), b16),
            pltpu.VMEM((PARTS, 512, 512), f32),
            pltpu.VMEM((PARTS, 512, 512), f32),
            pltpu.VMEM((512, 512), f32),
            pltpu.VMEM((512, BLK), f32),
            pltpu.VMEM((4, 4 * CHUNK, 512), b16),
            pltpu.VMEM((4, 4 * CHUNK, 512), b16),
            pltpu.VMEM((TAIL, 512), b16),
            pltpu.SemaphoreType.DMA((PARTS,)),
            pltpu.SemaphoreType.DMA((9,)),
        ],
        compiler_params=pltpu.CompilerParams(vmem_limit_bytes=52 << 20),
        cost_estimate=pl.CostEstimate(
            flops=12 * 10**9, bytes_accessed=18 * 10**6, transcendentals=3 * 10**6
        ),
    )(where, moved, seen, *weights, *parts)


def put_gains(ref, at, gains):
    high = gains.astype(jnp.bfloat16)
    low = (gains - high.astype(jnp.float32)).astype(jnp.bfloat16)
    ref[at : at + TAIL, :] = jnp.concatenate([high, low], axis=0)


def take_gains(ref, at):
    tail = ref[at : at + TAIL, :].astype(jnp.float32)
    return tail[: TAIL // 2] + tail[TAIL // 2 :]


def lift_far_kernel(keep, arrived, gains_ref, give, gains_out):
    rows = keep.shape[0]
    total = keep[...].astype(jnp.float32) + arrived[0:rows, :].astype(jnp.float32)
    give[0:rows, :] = total.astype(jnp.bfloat16)
    gains = add_gains(gains_ref[...], [take_gains(arrived, rows)])
    put_gains(give, rows, gains)
    gains_out[...] = gains


def lift_kernel(keep, arrived, gains_ref, give):
    rows = keep.shape[0]
    total = keep[...].astype(jnp.float32) + arrived[...].astype(jnp.float32)
    give[0:rows, :] = total.astype(jnp.bfloat16)
    put_gains(give, rows, gains_ref[...])


def quarters_kernel(where, keep, across, gains_ref, *refs):
    arrived, gives, own, gains_out = refs[:3], refs[3:6], refs[6], refs[7]
    for mask in range(4):
        at = pl.ds(pl.multiple_of((where[2] ^ mask) * CHUNK, CHUNK), CHUNK)
        value = keep[at, :].astype(jnp.float32) + across[at, :].astype(jnp.float32)
        for ref in arrived:
            value = value + ref[at, :].astype(jnp.float32)
        if mask:
            gives[mask - 1][0:CHUNK, :] = value.astype(jnp.bfloat16)
        else:
            own[...] = value
    gains = add_gains(gains_ref[...], [take_gains(ref, 4 * CHUNK) for ref in arrived])
    for give in gives:
        put_gains(give, CHUNK, gains)
    gains_out[...] = gains


def add_gains(own, arrived):
    high = own.astype(jnp.bfloat16).astype(jnp.float32)
    own = high + (own - high).astype(jnp.bfloat16).astype(jnp.float32)
    if len(arrived) == 1:
        return own + arrived[0]
    return (own + arrived[0]) + (arrived[1] + arrived[2])


def chunk_kernel(own_ref, gains_ref, *refs):
    arrived, give = refs[:3], refs[3]
    rows = own_ref.shape[0]
    value = own_ref[...]
    for ref in arrived:
        value = value + ref[0:rows, :].astype(jnp.float32)
    give[0:rows, :] = value.astype(jnp.bfloat16)
    put_gains(give, rows, add_gains(gains_ref[...], [take_gains(ref, rows) for ref in arrived]))


def last_kernel(own_ref, *refs):
    arrived, chunk, gains = refs[:3], refs[3], refs[4]
    rows = chunk.shape[0]
    a, b, c, d = (ref[0:rows, :].astype(jnp.float32) for ref in (own_ref, *arrived))
    chunk[...] = ((a + b) + (c + d)).astype(jnp.bfloat16)
    a, b, c, d = (take_gains(ref, rows) for ref in (own_ref, *arrived))
    put_gains(gains, 0, (a + b) + (c + d))


def arrange_kernel(where, gains, *refs):
    chunks, out = refs[:4], refs[4]
    for mask, chunk in enumerate(chunks):
        for at, rows in LAYOUT:
            to = pl.multiple_of(at * 4 + (where[2] ^ mask) * rows, 16)
            out[pl.ds(to, rows), :] = chunk[at : at + rows, :]
    out[4 * CHUNK :, :] = gains[...]


def place_kernel(which, where, *refs):
    count = len(which)
    arranged, grads, sems = refs[:count], refs[-7:-1], refs[-1]
    copies = []
    for i, (side, mask) in enumerate(which):
        holder = where[0] ^ side
        part = holder * 4 + (where[1 + side] ^ mask)
        for j, (at, rows) in enumerate(LAYOUT):
            to = pl.ds(pl.multiple_of(part * (4 * rows), 64), 4 * rows)
            grad = grads[min(j, 4 if j < 6 else 5)]
            target = grad.at[to, pl.ds(512 * (j - 4), 512)] if j in (4, 5) else grad.at[to, :]
            copies.append(
                pltpu.make_async_copy(arranged[i].at[pl.ds(at * 4, 4 * rows)], target, sems.at[i, j])
            )
    for copy in copies:
        copy.start()
    for copy in copies:
        copy.wait()


def place(which, where, arranged, grads):
    shapes = [(512, 512)] * 4 + [(512, 1024), (1024, 512)]
    count = len(which)
    return pl.pallas_call(
        lambda *refs: place_kernel(which, *refs),
        out_shape=[jax.ShapeDtypeStruct(shape, jnp.bfloat16) for shape in shapes],
        in_specs=[SMEM] + [ANY] * (count + len(grads)),
        out_specs=[ANY] * 6,
        scratch_shapes=[pltpu.SemaphoreType.DMA((count, len(LAYOUT)))],
        input_output_aliases={1 + count + i: i for i in range(len(grads))},
    )(where, *arranged, *grads)


def gains_kernel(where, own, other, gain_attn, gain_mlp):
    gains = jnp.where(where[0] == 0, take_gains(own, 4 * CHUNK), take_gains(other, 4 * CHUNK))
    gain_attn[...] = gains[0].astype(jnp.bfloat16)
    gain_mlp[...] = gains[1].astype(jnp.bfloat16)


def call(kernel, outs, *operands, scalars=0):
    return pl.pallas_call(
        kernel,
        out_shape=[jax.ShapeDtypeStruct(shape, dtype) for shape, dtype in outs],
        in_specs=[SMEM] * scalars + [VMEM] * (len(operands) - scalars),
        out_specs=[VMEM] * len(outs),
        compiler_params=pltpu.CompilerParams(vmem_limit_bytes=24 << 20),
    )(*operands)


def to_peers(give_of, route):
    return dict(sorted((mask, send(give_of(mask), route(mask))) for mask in ORDER))


def sum_everywhere(where, output, gains, *quarters):
    gives, keeps = quarters[:4], quarters[4:]
    b16, f32 = jnp.bfloat16, jnp.float32
    message = ((4 * CHUNK + TAIL, 512), b16)

    across = {mask: send(gives[mask], CORE) for mask in ORDER + (0,)}
    far, gains = call(lift_far_kernel, [message, ((8, 512), f32)], keeps[FAR], across[FAR], gains)

    def lifted(mask):
        if mask == FAR:
            return far
        return call(lift_kernel, [message], keeps[mask], across[mask], gains)[0]

    arrived = to_peers(lifted, first).values()
    output, *arrived = lax.optimization_barrier((send(output, SWAP), *arrived))
    small = ((CHUNK + TAIL, 512), b16)
    *gives, own, gains = call(
        quarters_kernel,
        [small] * 3 + [((CHUNK, 512), f32), ((8, 512), f32)],
        where, keeps[0], across[0], gains, *arrived, scalars=1,
    )
    arrived = to_peers(lambda mask: gives[mask - 1], second).values()
    (give,) = call(chunk_kernel, [small], own, gains, *arrived)
    arrived = to_peers(lambda mask: give, along_x).values()
    chunk, gains = call(last_kernel, [((CHUNK, 512), b16), ((TAIL, 512), b16)], give, *arrived)

    chunks = [chunk, *to_peers(lambda mask: chunk, second).values()]
    (mine,) = call(arrange_kernel, [message], where, gains, *chunks, scalars=1)
    own = {0: mine, **to_peers(lambda mask: mine, first)}
    other = {mask: send(own[mask], CORE) for mask in (0,) + ORDER}
    early = [(side, mask) for mask in (0,) + ORDER[:2] for side in range(2)]
    held = [(own, other)[side][mask] for side, mask in early]
    *held, last = lax.optimization_barrier((*held, own[ORDER[2]]))
    grads = place(early, where, held, ())
    grads = place([(0, ORDER[2]), (1, ORDER[2])], where, [last, other[ORDER[2]]], grads)
    gains = call(
        gains_kernel, [((512,), b16)] * 2, where, held[0], held[1], scalars=1
    )
    return (output[None], *grads, *gains)


def gather_features(own, others):
    near = {mask: send(own, first_swapped(mask)) for mask in (0,) + ORDER}
    mine = jnp.concatenate([near[mask] for mask in range(4)])
    mine, others = lax.optimization_barrier((mine, others))
    group = [mine, *to_peers(lambda mask: mine, second).values()]
    parts = group + [send(part, CORE) for part in group]
    core, y, z = (lax.axis_index(name) for name in ("core", "y", "z"))
    side, two, one = (jnp.asarray(i) for i in np.unravel_index(np.arange(32), (2, 4, 4)))
    holder = core ^ side
    block_y = jnp.where(holder == 0, y ^ one, y ^ two)
    block_z = jnp.where(holder == 0, z ^ two, z ^ one)
    return parts, block_z * 8 + holder * 4 + block_y, send(others, SWAP)


def local(
    queries,
    features,
    visible,
    cotangent,
    w_query,
    w_key,
    w_value,
    w_out,
    w_up,
    w_down,
    gain_attn,
    gain_mlp,
):
    seen = jnp.pad(visible[0].astype(jnp.bfloat16), ((0, 15), (0, 512 - visible.shape[-1])))
    parts, blocks, moved = gather_features(
        features[0], jnp.concatenate([queries[0], cotangent[0], seen])
    )
    seen = jnp.take(moved[2 * BLK].astype(jnp.float32), blocks)
    core, y, z = (lax.axis_index(name).astype(jnp.int32) for name in ("core", "y", "z"))
    where = jnp.stack([core, jnp.where(core == 0, y, z), jnp.where(core == 0, z, y)])
    return sum_everywhere(
        where,
        *device_step(
            where,
            moved,
            jnp.repeat(seen, BLK).reshape(PARTS, 512),
            parts,
            (w_query, w_key, w_value, w_out, w_up, w_down, gain_attn[None], gain_mlp[None]),
        )
    )


def solution(mesh):
    parts = Mesh(mesh.devices.reshape(SIZES), AXES)
    split = P(ROOM, GEOM, None)
    return jax.shard_map(
        local,
        mesh=parts,
        in_specs=(split,) * 4 + (P(),) * 8,
        out_specs=(split,) + (P(),) * 8,
        check_vma=False,
    )
```

```python
import math

import jax
import jax.numpy as jnp
import numpy as np
from jax import lax
from jax.experimental import pallas as pl
from jax.experimental.pallas import tpu as pltpu
from jax.sharding import Mesh, PartitionSpec as P

HEADS = 4
BLK = 128
EPSILON = 1e-05
GELU_COEF = math.sqrt(2.0 / math.pi)

AXES = ("x_hi", "core", "z", "x_lo", "y")
SIZES = (2, 2, 4, 2, 4)
ROOM = ("x_hi", "core")
GEOM = ("z", "x_lo", "y")
VMEM = pl.BlockSpec(memory_space=pltpu.VMEM)
SMEM = pl.BlockSpec(memory_space=pltpu.SMEM)
ANY = pl.BlockSpec(memory_space=pl.ANY)
FAR = 2
ORDER = (2, 1, 3)


def pairs_of(move):
    pairs = []
    for source in range(math.prod(SIZES)):
        target = move(*(int(i) for i in np.unravel_index(source, SIZES)))
        pairs.append((source, int(np.ravel_multi_index(target, SIZES))))
    return pairs


SWAP = pairs_of(lambda xh, c, z, xl, y: (xh, xl, z, c, y))
CORE = pairs_of(lambda xh, c, z, xl, y: (xh, 1 - c, z, xl, y))


def first(mask):
    return pairs_of(
        lambda xh, c, z, xl, y: (xh, c, z, xl, y ^ mask) if c == 0 else (xh, c, z ^ mask, xl, y)
    )


def first_swapped(mask):
    after = dict(first(mask))
    return [(source, after[target]) for source, target in SWAP]


def second(mask):
    return pairs_of(
        lambda xh, c, z, xl, y: (xh, c, z ^ mask, xl, y) if c == 0 else (xh, c, z, xl, y ^ mask)
    )


def along_x(mask):
    return pairs_of(lambda xh, c, z, xl, y: (xh ^ (mask >> 1), c, z, xl ^ (mask & 1), y))


def send(value, pairs):
    return lax.ppermute(value, AXES, pairs)


def normalize(inputs, gain):
    center = inputs - jnp.mean(inputs, axis=-1, keepdims=True)
    inverse = lax.rsqrt(jnp.mean(center * center, axis=-1, keepdims=True) + EPSILON)
    scaled = center * inverse
    return (scaled, inverse, scaled * gain)


def gelu_pair(inputs):
    inner = GELU_COEF * (inputs + 0.044715 * inputs * inputs * inputs)
    tangent = jnp.tanh(inner)
    value = 0.5 * inputs * (1.0 + tangent)
    slope = 0.5 * (1.0 + tangent) + 0.5 * inputs * (1.0 - tangent * tangent) * GELU_COEF * (
        1.0 + 3.0 * 0.044715 * inputs * inputs
    )
    return (value, slope)


def mult(left, right):
    return jnp.dot(left, right, preferred_element_type=jnp.float32)


def mult_nt(left, right):
    return lax.dot_general(
        left, right, (((1,), (1,)), ((), ())), preferred_element_type=jnp.float32
    )


def mult_tn(left, right):
    return lax.dot_general(
        left, right, (((0,), (0,)), ((), ())), preferred_element_type=jnp.float32
    )


def two_parts(value):
    high = value.astype(jnp.bfloat16)
    low = (value - high.astype(jnp.float32)).astype(jnp.bfloat16)
    return high, low


PARTS = 8
PIECES = 32
CHUNK = 128
TAIL = 16
LAYOUT = ((0, 16), (16, 16), (32, 16), (48, 16), (64, 16), (80, 16), (96, 32))


def lanes(value, combine):
    out = value[:, 0:BLK]
    for at in range(BLK, value.shape[1], BLK):
        out = combine(out, value[:, at : at + BLK])
    return out


def step_kernel(where, moved, seen, packed, w_up, w_down, gain_attn, gain_mlp, *refs):
    parts, (output, gains_out), refs = refs[:PARTS], refs[PARTS : PARTS + 2], refs[PARTS + 2 :]
    gives, keeps, refs = refs[:4], refs[4:8], refs[8:]
    scores, pulls, sums, stat, give, keep, tail, out_sems = refs
    f32, b16 = jnp.float32, jnp.bfloat16
    width = w_up.shape[0]
    w_query, w_key, w_value, w_out = (packed.at[pl.ds(i * width, width)] for i in range(4))
    head = width // HEADS
    factor = 1.0 / math.sqrt(head)
    cols = [slice(h * head, (h + 1) * head) for h in range(HEADS)]
    heads = [slice(h * BLK, (h + 1) * BLK) for h in range(HEADS)]
    inputs = moved[0:BLK, :].astype(f32)
    scaled_one, _, normed = normalize(inputs, gain_attn[...])
    normed_b = normed.astype(b16)
    query_rows = mult(normed_b, w_query[...]).astype(b16)

    blank = jnp.zeros((BLK, head), b16)
    query_pairs = jnp.concatenate(
        [
            jnp.concatenate(
                [query_rows[:, c] if h % 2 == side else blank for side in range(2)], axis=1
            )
            for h, c in enumerate(cols)
        ],
        axis=0,
    )
    pair_rows = [slice(0, 2 * BLK), slice(2 * BLK, 4 * BLK)]
    pair_cols = [slice(0, 2 * head), slice(2 * head, 4 * head)]

    stat[...] = jnp.full_like(stat, -1e30)

    for p in range(PARTS):
        key_rows = mult(parts[p][...], w_key[...]).astype(b16)
        allowed = seen[p : p + 1, :] > 0
        for r, c in zip(pair_rows, pair_cols):
            part = mult_nt(query_pairs[r, :], key_rows[:, c]) * factor
            part = jnp.where(allowed, part, -1e30)
            scores[p, r, :] = part
            stat[r, :] = jnp.maximum(stat[r, :], lanes(part, jnp.maximum))

    highest = jnp.max(stat[...], axis=-1, keepdims=True)
    stat[...] = jnp.zeros_like(stat)

    for p in range(PARTS):
        part = jnp.exp(scores[p] - highest)
        scores[p] = part
        stat[...] += lanes(part, jnp.add)

    inverse_sum = 1.0 / jnp.sum(stat[...], axis=-1, keepdims=True)
    sums[...] = jnp.zeros_like(sums)

    for p in range(PARTS):
        part = scores[p] * inverse_sum
        scores[p] = part
        sums[...] += mult(part.astype(b16), parts[p][...])

    u_high, u_low = two_parts(sums[...])
    context = jnp.concatenate(
        [mult(u_high[r], w_value[:, c]) + mult(u_low[r], w_value[:, c]) for r, c in zip(heads, cols)],
        axis=1,
    ).astype(b16)

    core = where[0]
    half = PIECES // 2

    def store(at, rows, grad):
        middle = grad.shape[0] // 2
        low, high = grad[:middle], grad[middle:]
        mine = jnp.where(core == 0, low, high).astype(b16)
        yours = jnp.where(core == 0, high, low).astype(b16)
        for i in range(half):
            row = i % 4 * CHUNK + at
            keep[i // 4, row : row + rows, :] = mine[i * rows : (i + 1) * rows]
            give[i // 4, row : row + rows, :] = yours[i * rows : (i + 1) * rows]

    mixed = inputs + mult(context, w_out[...])
    scaled_two, inverse_two, normed_two = normalize(mixed, gain_mlp[...])
    normed_two_b = normed_two.astype(b16)
    activated, slope = gelu_pair(mult(normed_two_b, w_up[...]))
    activated_b = activated.astype(b16)
    output[...] = (mixed + mult(activated_b, w_down[...])).astype(b16)
    cotangent = moved[BLK : 2 * BLK, :]
    store(96, 32, mult_tn(activated_b, cotangent))
    grad_upper_b = (mult_nt(cotangent, w_down[...]) * slope).astype(b16)
    store(64, 16, mult_tn(normed_two_b, grad_upper_b[:, :width]))
    store(80, 16, mult_tn(normed_two_b, grad_upper_b[:, width:]))
    grad_normed_two = mult_nt(grad_upper_b, w_up[...])
    grad_gain_mlp = jnp.sum(grad_normed_two * scaled_two, axis=0, keepdims=True)
    grad_scaled = grad_normed_two * gain_mlp[...]
    mean_one = jnp.mean(grad_scaled, axis=-1, keepdims=True)
    mean_two = jnp.mean(grad_scaled * scaled_two, axis=-1, keepdims=True)
    grad_mixed = cotangent.astype(f32) + inverse_two * (
        grad_scaled - mean_one - scaled_two * mean_two
    )
    grad_mixed_b = grad_mixed.astype(b16)
    store(48, 16, mult_tn(context, grad_mixed_b))
    grad_context = mult_nt(grad_mixed_b, w_out[...]).astype(b16)
    store(
        32,
        16,
        jnp.concatenate(
            [
                mult_tn(u_high[r], grad_context[:, c]) + mult_tn(u_low[r], grad_context[:, c])
                for r, c in zip(heads, cols)
            ],
            axis=1,
        ),
    )
    pulled = jnp.concatenate(
        [mult_nt(grad_context[:, c], w_value[:, c]) for c in cols], axis=0
    ).astype(b16)
    stat[...] = jnp.zeros_like(stat)

    for p in range(PARTS):
        part = mult_nt(pulled, parts[p][...])
        pulls[p] = part
        stat[...] += lanes(part * scores[p], jnp.add)

    centre = jnp.sum(stat[...], axis=-1, keepdims=True)
    sums[...] = jnp.zeros_like(sums)

    for p in range(PARTS):
        part = (scores[p] * (pulls[p] - centre) * factor).astype(b16)
        sums[...] += mult(part, parts[p][...])

    t_high, t_low = two_parts(sums[...])
    grad_query_rows = jnp.concatenate(
        [mult(t_high[r], w_key[:, c]) + mult(t_low[r], w_key[:, c]) for r, c in zip(heads, cols)],
        axis=1,
    ).astype(b16)
    store(
        16,
        16,
        jnp.concatenate(
            [
                mult_tn(t_high[r], query_rows[:, c]) + mult_tn(t_low[r], query_rows[:, c])
                for r, c in zip(heads, cols)
            ],
            axis=1,
        ),
    )
    store(0, 16, mult_tn(normed_b, grad_query_rows))
    grad_normed = mult_nt(grad_query_rows, w_query[...])
    grad_gain_attn = jnp.sum(grad_normed * scaled_one, axis=0, keepdims=True)
    gains = jnp.concatenate([grad_gain_attn, grad_gain_mlp, jnp.zeros((6, width), f32)], axis=0)
    put_gains(tail, 0, gains)
    gains_out[...] = gains
    one, two = where[1], where[2]
    copies = [
        pltpu.make_async_copy(tail, gives[FAR].at[pl.ds(4 * CHUNK, TAIL)], out_sems.at[8])
    ]
    for i, mask in enumerate(ORDER + (0,)):
        for j, (held, outs, index) in enumerate(((give, gives, two), (keep, keeps, one))):
            copies.append(
                pltpu.make_async_copy(
                    held.at[index ^ mask],
                    outs[mask].at[pl.ds(0, 4 * CHUNK)],
                    out_sems.at[2 * i + j],
                )
            )
    for copy in copies:
        copy.start()
    for copy in copies:
        copy.wait()


def device_step(where, moved, seen, parts, weights):
    f32, b16 = jnp.float32, jnp.bfloat16
    quarters = [(4 * CHUNK + (TAIL if mask == FAR else 0), 512) for mask in range(4)]
    return pl.pallas_call(
        step_kernel,
        out_shape=[
            jax.ShapeDtypeStruct((BLK, 512), b16),
            jax.ShapeDtypeStruct((8, 512), f32),
        ]
        + [jax.ShapeDtypeStruct(shape, b16) for shape in quarters]
        + [jax.ShapeDtypeStruct((4 * CHUNK, 512), b16)] * 4,
        in_specs=[SMEM] + [VMEM] * (7 + PARTS),
        out_specs=[VMEM] * 2 + [ANY] * 8,
        scratch_shapes=[
            pltpu.VMEM((PARTS, 512, 512), f32),
            pltpu.VMEM((PARTS, 512, 512), f32),
            pltpu.VMEM((512, 512), f32),
            pltpu.VMEM((512, BLK), f32),
            pltpu.VMEM((4, 4 * CHUNK, 512), b16),
            pltpu.VMEM((4, 4 * CHUNK, 512), b16),
            pltpu.VMEM((TAIL, 512), b16),
            pltpu.SemaphoreType.DMA((9,)),
        ],
        compiler_params=pltpu.CompilerParams(vmem_limit_bytes=38 << 20),
        cost_estimate=pl.CostEstimate(
            flops=12 * 10**9, bytes_accessed=18 * 10**6, transcendentals=3 * 10**6
        ),
    )(where, moved, seen, *weights, *parts)


def put_gains(ref, at, gains):
    high = gains.astype(jnp.bfloat16)
    low = (gains - high.astype(jnp.float32)).astype(jnp.bfloat16)
    ref[at : at + TAIL, :] = jnp.concatenate([high, low], axis=0)


def take_gains(ref, at):
    tail = ref[at : at + TAIL, :].astype(jnp.float32)
    return tail[: TAIL // 2] + tail[TAIL // 2 :]


def lift_far_kernel(keep, arrived, gains_ref, give, gains_out):
    rows = keep.shape[0]
    total = keep[...].astype(jnp.float32) + arrived[0:rows, :].astype(jnp.float32)
    give[0:rows, :] = total.astype(jnp.bfloat16)
    gains = add_gains(gains_ref[...], [take_gains(arrived, rows)])
    put_gains(give, rows, gains)
    gains_out[...] = gains


def lift_kernel(keep, arrived, gains_ref, give):
    rows = keep.shape[0]
    total = keep[...].astype(jnp.float32) + arrived[...].astype(jnp.float32)
    give[0:rows, :] = total.astype(jnp.bfloat16)
    put_gains(give, rows, gains_ref[...])


def quarters_kernel(where, keep, across, gains_ref, *refs):
    arrived, gives, own, gains_out = refs[:3], refs[3:6], refs[6], refs[7]
    for mask in range(4):
        at = pl.ds(pl.multiple_of((where[2] ^ mask) * CHUNK, CHUNK), CHUNK)
        value = keep[at, :].astype(jnp.float32) + across[at, :].astype(jnp.float32)
        for ref in arrived:
            value = value + ref[at, :].astype(jnp.float32)
        if mask:
            gives[mask - 1][0:CHUNK, :] = value.astype(jnp.bfloat16)
        else:
            own[...] = value
    gains = add_gains(gains_ref[...], [take_gains(ref, 4 * CHUNK) for ref in arrived])
    for give in gives:
        put_gains(give, CHUNK, gains)
    gains_out[...] = gains


def add_gains(own, arrived):
    high = own.astype(jnp.bfloat16).astype(jnp.float32)
    own = high + (own - high).astype(jnp.bfloat16).astype(jnp.float32)
    if len(arrived) == 1:
        return own + arrived[0]
    return (own + arrived[0]) + (arrived[1] + arrived[2])


def chunk_kernel(own_ref, gains_ref, *refs):
    arrived, give = refs[:3], refs[3]
    rows = own_ref.shape[0]
    value = own_ref[...]
    for ref in arrived:
        value = value + ref[0:rows, :].astype(jnp.float32)
    give[0:rows, :] = value.astype(jnp.bfloat16)
    put_gains(give, rows, add_gains(gains_ref[...], [take_gains(ref, rows) for ref in arrived]))


def last_kernel(own_ref, *refs):
    arrived, chunk, gains = refs[:3], refs[3], refs[4]
    rows = chunk.shape[0]
    a, b, c, d = (ref[0:rows, :].astype(jnp.float32) for ref in (own_ref, *arrived))
    chunk[...] = ((a + b) + (c + d)).astype(jnp.bfloat16)
    a, b, c, d = (take_gains(ref, rows) for ref in (own_ref, *arrived))
    put_gains(gains, 0, (a + b) + (c + d))


def arrange_kernel(where, gains, *refs):
    chunks, out = refs[:4], refs[4]
    for mask, chunk in enumerate(chunks):
        for at, rows in LAYOUT:
            to = pl.multiple_of(at * 4 + (where[2] ^ mask) * rows, 16)
            out[pl.ds(to, rows), :] = chunk[at : at + rows, :]
    out[4 * CHUNK :, :] = gains[...]


def place_kernel(where, *refs):
    groups, grads, gain_attn, gain_mlp = (refs[0:4], refs[4:8]), refs[8:14], refs[14], refs[15]
    for side, group in enumerate(groups):
        holder = where[0] ^ side
        for mask, arranged in enumerate(group):
            part = holder * 4 + (where[1 + side] ^ mask)
            for j, (at, rows) in enumerate(LAYOUT):
                to = pl.ds(pl.multiple_of(part * (4 * rows), 64), 4 * rows)
                piece = arranged[at * 4 : (at + rows) * 4, :]
                if j in (4, 5):
                    grads[4][to, 512 * (j - 4) : 512 * (j - 3)] = piece
                else:
                    grads[min(j, 5)][to, :] = piece
    own, other = (take_gains(group[0], 4 * CHUNK) for group in groups)
    gains = jnp.where(where[0] == 0, own, other).astype(jnp.bfloat16)
    gain_attn[...] = gains[0]
    gain_mlp[...] = gains[1]


def call(kernel, outs, *operands, scalars=0):
    return pl.pallas_call(
        kernel,
        out_shape=[jax.ShapeDtypeStruct(shape, dtype) for shape, dtype in outs],
        in_specs=[SMEM] * scalars + [VMEM] * (len(operands) - scalars),
        out_specs=[VMEM] * len(outs),
        compiler_params=pltpu.CompilerParams(vmem_limit_bytes=24 << 20),
    )(*operands)


def to_peers(give_of, route):
    return dict(sorted((mask, send(give_of(mask), route(mask))) for mask in ORDER))


def sum_everywhere(where, output, gains, *quarters):
    gives, keeps = quarters[:4], quarters[4:]
    b16, f32 = jnp.bfloat16, jnp.float32
    message = ((4 * CHUNK + TAIL, 512), b16)

    across = {mask: send(gives[mask], CORE) for mask in ORDER + (0,)}
    far, gains = call(lift_far_kernel, [message, ((8, 512), f32)], keeps[FAR], across[FAR], gains)

    def lifted(mask):
        if mask == FAR:
            return far
        return call(lift_kernel, [message], keeps[mask], across[mask], gains)[0]

    arrived = to_peers(lifted, first).values()
    output, *arrived = lax.optimization_barrier((send(output, SWAP), *arrived))
    small = ((CHUNK + TAIL, 512), b16)
    *gives, own, gains = call(
        quarters_kernel,
        [small] * 3 + [((CHUNK, 512), f32), ((8, 512), f32)],
        where, keeps[0], across[0], gains, *arrived, scalars=1,
    )
    arrived = to_peers(lambda mask: gives[mask - 1], second).values()
    (give,) = call(chunk_kernel, [small], own, gains, *arrived)
    arrived = to_peers(lambda mask: give, along_x).values()
    chunk, gains = call(last_kernel, [((CHUNK, 512), b16), ((TAIL, 512), b16)], give, *arrived)

    chunks = [chunk, *to_peers(lambda mask: chunk, second).values()]
    (mine,) = call(arrange_kernel, [message], where, gains, *chunks, scalars=1)
    own = {0: mine, **to_peers(lambda mask: mine, first)}
    other = {mask: send(own[mask], CORE) for mask in (0,) + ORDER}
    placed = call(
        place_kernel,
        [((512, 512), b16)] * 4 + [((512, 1024), b16), ((1024, 512), b16)] + [((512,), b16)] * 2,
        where, *(own[mask] for mask in range(4)), *(other[mask] for mask in range(4)), scalars=1,
    )
    return (output[None], *placed)


def gather_features(own, others, weights):
    near = {mask: send(own, first_swapped(mask)) for mask in (0,) + ORDER}
    mine = jnp.concatenate([near[mask] for mask in range(4)])
    mine, others, weights = lax.optimization_barrier((mine, others, weights))
    group = [mine, *to_peers(lambda mask: mine, second).values()]
    parts = group + [send(part, CORE) for part in group]
    core, y, z = (lax.axis_index(name) for name in ("core", "y", "z"))
    side, two, one = (jnp.asarray(i) for i in np.unravel_index(np.arange(32), (2, 4, 4)))
    holder = core ^ side
    block_y = jnp.where(holder == 0, y ^ one, y ^ two)
    block_z = jnp.where(holder == 0, z ^ two, z ^ one)
    return parts, block_z * 8 + holder * 4 + block_y, send(others, SWAP), jnp.concatenate(weights)


def local(
    queries,
    features,
    visible,
    cotangent,
    w_query,
    w_key,
    w_value,
    w_out,
    w_up,
    w_down,
    gain_attn,
    gain_mlp,
):
    seen = jnp.pad(visible[0].astype(jnp.bfloat16), ((0, 15), (0, 512 - visible.shape[-1])))
    parts, blocks, moved, packed = gather_features(
        features[0],
        jnp.concatenate([queries[0], cotangent[0], seen]),
        (w_query, w_key, w_value, w_out),
    )
    seen = jnp.take(moved[2 * BLK].astype(jnp.float32), blocks)
    core, y, z = (lax.axis_index(name).astype(jnp.int32) for name in ("core", "y", "z"))
    where = jnp.stack([core, jnp.where(core == 0, y, z), jnp.where(core == 0, z, y)])
    return sum_everywhere(
        where,
        *device_step(
            where,
            moved,
            jnp.repeat(seen, BLK).reshape(PARTS, 512),
            parts,
            (packed, w_up, w_down, gain_attn[None], gain_mlp[None]),
        )
    )


def solution(mesh):
    parts = Mesh(mesh.devices.reshape(SIZES), AXES)
    split = P(ROOM, GEOM, None)
    return jax.shard_map(
        local,
        mesh=parts,
        in_specs=(split,) * 4 + (P(),) * 8,
        out_specs=(split,) + (P(),) * 8,
        check_vma=False,
    )
```

```python
import math

import jax
import jax.numpy as jnp
import numpy as np
from jax import lax
from jax.experimental import pallas as pl
from jax.experimental.pallas import tpu as pltpu
from jax.sharding import Mesh, PartitionSpec as P

HEADS = 4
BLK = 128
EPSILON = 1e-05
GELU_COEF = math.sqrt(2.0 / math.pi)

AXES = ("x_hi", "core", "z", "x_lo", "y")
SIZES = (2, 2, 4, 2, 4)
ROOM = ("x_hi", "core")
GEOM = ("z", "x_lo", "y")
VMEM = pl.BlockSpec(memory_space=pltpu.VMEM)
SMEM = pl.BlockSpec(memory_space=pltpu.SMEM)
ANY = pl.BlockSpec(memory_space=pl.ANY)
FAR = 2
ORDER = (2, 1, 3)


def pairs_of(move):
    pairs = []
    for source in range(math.prod(SIZES)):
        target = move(*(int(i) for i in np.unravel_index(source, SIZES)))
        pairs.append((source, int(np.ravel_multi_index(target, SIZES))))
    return pairs


SWAP = pairs_of(lambda xh, c, z, xl, y: (xh, xl, z, c, y))
CORE = pairs_of(lambda xh, c, z, xl, y: (xh, 1 - c, z, xl, y))


def first(mask):
    return pairs_of(
        lambda xh, c, z, xl, y: (xh, c, z, xl, y ^ mask) if c == 0 else (xh, c, z ^ mask, xl, y)
    )


def first_swapped(mask):
    after = dict(first(mask))
    return [(source, after[target]) for source, target in SWAP]


def second(mask):
    return pairs_of(
        lambda xh, c, z, xl, y: (xh, c, z ^ mask, xl, y) if c == 0 else (xh, c, z, xl, y ^ mask)
    )


def along_x(mask):
    return pairs_of(lambda xh, c, z, xl, y: (xh ^ (mask >> 1), c, z, xl ^ (mask & 1), y))


def send(value, pairs):
    return lax.ppermute(value, AXES, pairs)


def normalize(inputs, gain):
    center = inputs - jnp.mean(inputs, axis=-1, keepdims=True)
    inverse = lax.rsqrt(jnp.mean(center * center, axis=-1, keepdims=True) + EPSILON)
    scaled = center * inverse
    return (scaled, inverse, scaled * gain)


def gelu_pair(inputs):
    inner = GELU_COEF * (inputs + 0.044715 * inputs * inputs * inputs)
    tangent = jnp.tanh(inner)
    value = 0.5 * inputs * (1.0 + tangent)
    slope = 0.5 * (1.0 + tangent) + 0.5 * inputs * (1.0 - tangent * tangent) * GELU_COEF * (
        1.0 + 3.0 * 0.044715 * inputs * inputs
    )
    return (value, slope)


def mult(left, right):
    return jnp.dot(left, right, preferred_element_type=jnp.float32)


def mult_nt(left, right):
    return lax.dot_general(
        left, right, (((1,), (1,)), ((), ())), preferred_element_type=jnp.float32
    )


def mult_tn(left, right):
    return lax.dot_general(
        left, right, (((0,), (0,)), ((), ())), preferred_element_type=jnp.float32
    )


def two_parts(value):
    high = value.astype(jnp.bfloat16)
    low = (value - high.astype(jnp.float32)).astype(jnp.bfloat16)
    return high, low


PARTS = 8
PIECES = 32
CHUNK = 128
TAIL = 16
LAYOUT = ((0, 16), (16, 16), (32, 16), (48, 16), (64, 16), (80, 16), (96, 32))


def lanes(value, combine):
    out = value[:, 0:BLK]
    for at in range(BLK, value.shape[1], BLK):
        out = combine(out, value[:, at : at + BLK])
    return out


def step_kernel(where, moved, seen, packed, w_up, w_down, gain_attn, gain_mlp, *refs):
    parts, (output, gains_out), refs = refs[:PARTS], refs[PARTS : PARTS + 2], refs[PARTS + 2 :]
    gives, keeps, refs = refs[:4], refs[4:8], refs[8:]
    scores, pulls, sums, stat, give, keep, tail, out_sems = refs
    f32, b16 = jnp.float32, jnp.bfloat16
    width = w_up.shape[0]
    w_query, w_key, w_value, w_out = (packed.at[pl.ds(i * width, width)] for i in range(4))
    head = width // HEADS
    factor = 1.0 / math.sqrt(head)
    cols = [slice(h * head, (h + 1) * head) for h in range(HEADS)]
    heads = [slice(h * BLK, (h + 1) * BLK) for h in range(HEADS)]
    inputs = moved[0:BLK, :].astype(f32)
    scaled_one, _, normed = normalize(inputs, gain_attn[...])
    normed_b = normed.astype(b16)
    query_rows = mult(normed_b, w_query[...]).astype(b16)

    blank = jnp.zeros((BLK, head), b16)
    query_pairs = jnp.concatenate(
        [
            jnp.concatenate(
                [query_rows[:, c] if h % 2 == side else blank for side in range(2)], axis=1
            )
            for h, c in enumerate(cols)
        ],
        axis=0,
    )
    pair_rows = [slice(0, 2 * BLK), slice(2 * BLK, 4 * BLK)]
    pair_cols = [slice(0, 2 * head), slice(2 * head, 4 * head)]

    stat[...] = jnp.full_like(stat, -1e30)

    for p in range(PARTS):
        key_rows = mult(parts[p][...], w_key[...]).astype(b16)
        allowed = seen[p : p + 1, :] > 0
        for r, c in zip(pair_rows, pair_cols):
            part = mult_nt(query_pairs[r, :], key_rows[:, c]) * factor
            part = jnp.where(allowed, part, -1e30)
            scores[p, r, :] = part
            stat[r, :] = jnp.maximum(stat[r, :], lanes(part, jnp.maximum))

    highest = jnp.max(stat[...], axis=-1, keepdims=True)
    stat[...] = jnp.zeros_like(stat)

    for p in range(PARTS):
        part = jnp.exp(scores[p] - highest)
        scores[p] = part
        stat[...] += lanes(part, jnp.add)

    inverse_sum = 1.0 / jnp.sum(stat[...], axis=-1, keepdims=True)
    sums[...] = jnp.zeros_like(sums)

    for p in range(PARTS):
        part = scores[p] * inverse_sum
        scores[p] = part
        sums[...] += mult(part.astype(b16), parts[p][...])

    u_high, u_low = two_parts(sums[...])
    context = jnp.concatenate(
        [mult(u_high[r], w_value[:, c]) + mult(u_low[r], w_value[:, c]) for r, c in zip(heads, cols)],
        axis=1,
    ).astype(b16)

    core = where[0]
    half = PIECES // 2

    def store(at, rows, grad):
        middle = grad.shape[0] // 2
        low, high = grad[:middle], grad[middle:]
        mine = jnp.where(core == 0, low, high).astype(b16)
        yours = jnp.where(core == 0, high, low).astype(b16)
        for i in range(half):
            row = i % 4 * CHUNK + at
            keep[i // 4, row : row + rows, :] = mine[i * rows : (i + 1) * rows]
            give[i // 4, row : row + rows, :] = yours[i * rows : (i + 1) * rows]

    mixed = inputs + mult(context, w_out[...])
    scaled_two, inverse_two, normed_two = normalize(mixed, gain_mlp[...])
    normed_two_b = normed_two.astype(b16)
    activated, slope = gelu_pair(mult(normed_two_b, w_up[...]))
    activated_b = activated.astype(b16)
    output[...] = (mixed + mult(activated_b, w_down[...])).astype(b16)
    cotangent = moved[BLK : 2 * BLK, :]
    store(96, 32, mult_tn(activated_b, cotangent))
    grad_upper_b = (mult_nt(cotangent, w_down[...]) * slope).astype(b16)
    store(64, 16, mult_tn(normed_two_b, grad_upper_b[:, :width]))
    store(80, 16, mult_tn(normed_two_b, grad_upper_b[:, width:]))
    grad_normed_two = mult_nt(grad_upper_b, w_up[...])
    grad_gain_mlp = jnp.sum(grad_normed_two * scaled_two, axis=0, keepdims=True)
    grad_scaled = grad_normed_two * gain_mlp[...]
    mean_one = jnp.mean(grad_scaled, axis=-1, keepdims=True)
    mean_two = jnp.mean(grad_scaled * scaled_two, axis=-1, keepdims=True)
    grad_mixed = cotangent.astype(f32) + inverse_two * (
        grad_scaled - mean_one - scaled_two * mean_two
    )
    grad_mixed_b = grad_mixed.astype(b16)
    store(48, 16, mult_tn(context, grad_mixed_b))
    grad_context = mult_nt(grad_mixed_b, w_out[...]).astype(b16)
    store(
        32,
        16,
        jnp.concatenate(
            [
                mult_tn(u_high[r], grad_context[:, c]) + mult_tn(u_low[r], grad_context[:, c])
                for r, c in zip(heads, cols)
            ],
            axis=1,
        ),
    )
    pulled = jnp.concatenate(
        [mult_nt(grad_context[:, c], w_value[:, c]) for c in cols], axis=0
    ).astype(b16)
    stat[...] = jnp.zeros_like(stat)

    for p in range(PARTS):
        part = mult_nt(pulled, parts[p][...])
        pulls[p] = part
        stat[...] += lanes(part * scores[p], jnp.add)

    centre = jnp.sum(stat[...], axis=-1, keepdims=True)
    sums[...] = jnp.zeros_like(sums)

    for p in range(PARTS):
        part = (scores[p] * (pulls[p] - centre) * factor).astype(b16)
        sums[...] += mult(part, parts[p][...])

    t_high, t_low = two_parts(sums[...])
    grad_query_rows = jnp.concatenate(
        [mult(t_high[r], w_key[:, c]) + mult(t_low[r], w_key[:, c]) for r, c in zip(heads, cols)],
        axis=1,
    ).astype(b16)
    store(
        16,
        16,
        jnp.concatenate(
            [
                mult_tn(t_high[r], query_rows[:, c]) + mult_tn(t_low[r], query_rows[:, c])
                for r, c in zip(heads, cols)
            ],
            axis=1,
        ),
    )
    store(0, 16, mult_tn(normed_b, grad_query_rows))
    grad_normed = mult_nt(grad_query_rows, w_query[...])
    grad_gain_attn = jnp.sum(grad_normed * scaled_one, axis=0, keepdims=True)
    gains = jnp.concatenate([grad_gain_attn, grad_gain_mlp, jnp.zeros((6, width), f32)], axis=0)
    put_gains(tail, 0, gains)
    gains_out[...] = gains
    one, two = where[1], where[2]
    copies = [
        pltpu.make_async_copy(tail, gives[FAR].at[pl.ds(4 * CHUNK, TAIL)], out_sems.at[8])
    ]
    for i, mask in enumerate(ORDER + (0,)):
        for j, (held, outs, index) in enumerate(((give, gives, two), (keep, keeps, one))):
            copies.append(
                pltpu.make_async_copy(
                    held.at[index ^ mask],
                    outs[mask].at[pl.ds(0, 4 * CHUNK)],
                    out_sems.at[2 * i + j],
                )
            )
    for copy in copies:
        copy.start()
    for copy in copies:
        copy.wait()


def device_step(where, moved, seen, parts, weights):
    f32, b16 = jnp.float32, jnp.bfloat16
    quarters = [(4 * CHUNK + (TAIL if mask == FAR else 0), 512) for mask in range(4)]
    return pl.pallas_call(
        step_kernel,
        out_shape=[
            jax.ShapeDtypeStruct((BLK, 512), b16),
            jax.ShapeDtypeStruct((8, 512), f32),
        ]
        + [jax.ShapeDtypeStruct(shape, b16) for shape in quarters]
        + [jax.ShapeDtypeStruct((4 * CHUNK, 512), b16)] * 4,
        in_specs=[SMEM] + [VMEM] * (7 + PARTS),
        out_specs=[VMEM] * 2 + [ANY] * 8,
        scratch_shapes=[
            pltpu.VMEM((PARTS, 512, 512), f32),
            pltpu.VMEM((PARTS, 512, 512), f32),
            pltpu.VMEM((512, 512), f32),
            pltpu.VMEM((512, BLK), f32),
            pltpu.VMEM((4, 4 * CHUNK, 512), b16),
            pltpu.VMEM((4, 4 * CHUNK, 512), b16),
            pltpu.VMEM((TAIL, 512), b16),
            pltpu.SemaphoreType.DMA((9,)),
        ],
        compiler_params=pltpu.CompilerParams(vmem_limit_bytes=38 << 20),
        cost_estimate=pl.CostEstimate(
            flops=12 * 10**9, bytes_accessed=18 * 10**6, transcendentals=3 * 10**6
        ),
    )(where, moved, seen, *weights, *parts)


def put_gains(ref, at, gains):
    high = gains.astype(jnp.bfloat16)
    low = (gains - high.astype(jnp.float32)).astype(jnp.bfloat16)
    ref[at : at + TAIL, :] = jnp.concatenate([high, low], axis=0)


def take_gains(ref, at):
    tail = ref[at : at + TAIL, :].astype(jnp.float32)
    return tail[: TAIL // 2] + tail[TAIL // 2 :]


def lift_far_kernel(keep, arrived, gains_ref, give, gains_out):
    rows = keep.shape[0]
    total = keep[...].astype(jnp.float32) + arrived[0:rows, :].astype(jnp.float32)
    give[0:rows, :] = total.astype(jnp.bfloat16)
    gains = add_gains(gains_ref[...], [take_gains(arrived, rows)])
    put_gains(give, rows, gains)
    gains_out[...] = gains


def lift_kernel(keep, arrived, gains_ref, give):
    rows = keep.shape[0]
    total = keep[...].astype(jnp.float32) + arrived[...].astype(jnp.float32)
    give[0:rows, :] = total.astype(jnp.bfloat16)
    put_gains(give, rows, gains_ref[...])


def quarters_kernel(where, keep, across, gains_ref, *refs):
    arrived, gives, own, gains_out = refs[:3], refs[3:6], refs[6], refs[7]
    for mask in range(4):
        at = pl.ds(pl.multiple_of((where[2] ^ mask) * CHUNK, CHUNK), CHUNK)
        value = keep[at, :].astype(jnp.float32) + across[at, :].astype(jnp.float32)
        for ref in arrived:
            value = value + ref[at, :].astype(jnp.float32)
        if mask:
            gives[mask - 1][0:CHUNK, :] = value.astype(jnp.bfloat16)
        else:
            own[...] = value
    gains = add_gains(gains_ref[...], [take_gains(ref, 4 * CHUNK) for ref in arrived])
    for give in gives:
        put_gains(give, CHUNK, gains)
    gains_out[...] = gains


def add_gains(own, arrived):
    high = own.astype(jnp.bfloat16).astype(jnp.float32)
    own = high + (own - high).astype(jnp.bfloat16).astype(jnp.float32)
    if len(arrived) == 1:
        return own + arrived[0]
    return (own + arrived[0]) + (arrived[1] + arrived[2])


def chunk_kernel(own_ref, gains_ref, *refs):
    arrived, give = refs[:3], refs[3]
    rows = own_ref.shape[0]
    value = own_ref[...]
    for ref in arrived:
        value = value + ref[0:rows, :].astype(jnp.float32)
    give[0:rows, :] = value.astype(jnp.bfloat16)
    put_gains(give, rows, add_gains(gains_ref[...], [take_gains(ref, rows) for ref in arrived]))


def last_kernel(own_ref, *refs):
    arrived, chunk, gains = refs[:3], refs[3], refs[4]
    rows = chunk.shape[0]
    a, b, c, d = (ref[0:rows, :].astype(jnp.float32) for ref in (own_ref, *arrived))
    chunk[...] = ((a + b) + (c + d)).astype(jnp.bfloat16)
    a, b, c, d = (take_gains(ref, rows) for ref in (own_ref, *arrived))
    put_gains(gains, 0, (a + b) + (c + d))


def arrange_kernel(where, gains, *refs):
    chunks, out = refs[:4], refs[4]
    for mask, chunk in enumerate(chunks):
        for at, rows in LAYOUT:
            to = pl.multiple_of(at * 4 + (where[2] ^ mask) * rows, 16)
            out[pl.ds(to, rows), :] = chunk[at : at + rows, :]
    out[4 * CHUNK :, :] = gains[...]


def place_kernel(where, *refs):
    groups, refs = (refs[0:4], refs[4:8]), refs[8:]
    output, output_out, grads, gain_attn, gain_mlp = refs[0], refs[1], refs[2:8], refs[8], refs[9]
    output_out[0] = output[...]
    for side, group in enumerate(groups):
        holder = where[0] ^ side
        for mask, arranged in enumerate(group):
            part = holder * 4 + (where[1 + side] ^ mask)
            for j, (at, rows) in enumerate(LAYOUT):
                to = pl.ds(pl.multiple_of(part * (4 * rows), 64), 4 * rows)
                piece = arranged[at * 4 : (at + rows) * 4, :]
                if j in (4, 5):
                    grads[4][to, 512 * (j - 4) : 512 * (j - 3)] = piece
                else:
                    grads[min(j, 5)][to, :] = piece
    own, other = (take_gains(group[0], 4 * CHUNK) for group in groups)
    gains = jnp.where(where[0] == 0, own, other).astype(jnp.bfloat16)
    gain_attn[...] = gains[0]
    gain_mlp[...] = gains[1]


def call(kernel, outs, *operands, scalars=0):
    return pl.pallas_call(
        kernel,
        out_shape=[jax.ShapeDtypeStruct(shape, dtype) for shape, dtype in outs],
        in_specs=[SMEM] * scalars + [VMEM] * (len(operands) - scalars),
        out_specs=[VMEM] * len(outs),
        compiler_params=pltpu.CompilerParams(vmem_limit_bytes=24 << 20),
    )(*operands)


def to_peers(give_of, route):
    return dict(sorted((mask, send(give_of(mask), route(mask))) for mask in ORDER))


def sum_everywhere(where, output, gains, *quarters):
    gives, keeps = quarters[:4], quarters[4:]
    b16, f32 = jnp.bfloat16, jnp.float32
    message = ((4 * CHUNK + TAIL, 512), b16)

    across = {mask: send(gives[mask], CORE) for mask in ORDER + (0,)}
    far, gains = call(lift_far_kernel, [message, ((8, 512), f32)], keeps[FAR], across[FAR], gains)

    def lifted(mask):
        if mask == FAR:
            return far
        return call(lift_kernel, [message], keeps[mask], across[mask], gains)[0]

    arrived = to_peers(lifted, first).values()
    output, *arrived = lax.optimization_barrier((send(output, SWAP), *arrived))
    small = ((CHUNK + TAIL, 512), b16)
    *gives, own, gains = call(
        quarters_kernel,
        [small] * 3 + [((CHUNK, 512), f32), ((8, 512), f32)],
        where, keeps[0], across[0], gains, *arrived, scalars=1,
    )
    arrived = to_peers(lambda mask: gives[mask - 1], second).values()
    (give,) = call(chunk_kernel, [small], own, gains, *arrived)
    arrived = to_peers(lambda mask: give, along_x).values()
    chunk, gains = call(last_kernel, [((CHUNK, 512), b16), ((TAIL, 512), b16)], give, *arrived)

    chunks = [chunk, *to_peers(lambda mask: chunk, second).values()]
    (mine,) = call(arrange_kernel, [message], where, gains, *chunks, scalars=1)
    own = {0: mine, **to_peers(lambda mask: mine, first)}
    other = {mask: send(own[mask], CORE) for mask in (0,) + ORDER}
    placed = call(
        place_kernel,
        [((1, BLK, 512), b16)]
        + [((512, 512), b16)] * 4
        + [((512, 1024), b16), ((1024, 512), b16)]
        + [((512,), b16)] * 2,
        where, *(own[mask] for mask in range(4)), *(other[mask] for mask in range(4)), output, scalars=1,
    )
    return tuple(placed)


def gather_features(own, others, seen, weights):
    near = {mask: send(own, first_swapped(mask)) for mask in (0,) + ORDER}
    mine = jnp.concatenate([near[mask] for mask in range(4)])
    mine, others, seen, weights = lax.optimization_barrier((mine, others, seen, weights))
    group = [mine, *to_peers(lambda mask: mine, second).values()]
    parts = group + [send(part, CORE) for part in group]
    core, y, z = (lax.axis_index(name) for name in ("core", "y", "z"))
    side, two, one = (jnp.asarray(i) for i in np.unravel_index(np.arange(32), (2, 4, 4)))
    holder = core ^ side
    block_y = jnp.where(holder == 0, y ^ one, y ^ two)
    block_z = jnp.where(holder == 0, z ^ two, z ^ one)
    others = jnp.concatenate([*others, jnp.pad(seen, ((0, 15), (0, 512 - seen.shape[-1])))])
    return parts, block_z * 8 + holder * 4 + block_y, send(others, SWAP), jnp.concatenate(weights)


def local(
    queries,
    features,
    visible,
    cotangent,
    w_query,
    w_key,
    w_value,
    w_out,
    w_up,
    w_down,
    gain_attn,
    gain_mlp,
):
    parts, blocks, moved, packed = gather_features(
        features[0],
        (queries[0], cotangent[0]),
        visible[0].astype(jnp.bfloat16),
        (w_query, w_key, w_value, w_out),
    )
    seen = jnp.take(moved[2 * BLK].astype(jnp.float32), blocks)
    core, y, z = (lax.axis_index(name).astype(jnp.int32) for name in ("core", "y", "z"))
    where = jnp.stack([core, jnp.where(core == 0, y, z), jnp.where(core == 0, z, y)])
    return sum_everywhere(
        where,
        *device_step(
            where,
            moved,
            jnp.repeat(seen, BLK).reshape(PARTS, 512),
            parts,
            (packed, w_up, w_down, gain_attn[None], gain_mlp[None]),
        )
    )


def solution(mesh):
    parts = Mesh(mesh.devices.reshape(SIZES), AXES)
    split = P(ROOM, GEOM, None)
    return jax.shard_map(
        local,
        mesh=parts,
        in_specs=(split,) * 4 + (P(),) * 8,
        out_specs=(split,) + (P(),) * 8,
        check_vma=False,
    )
```

```python
import math

import jax
import jax.numpy as jnp
import numpy as np
from jax import lax
from jax.experimental import pallas as pl
from jax.experimental.pallas import tpu as pltpu
from jax.sharding import Mesh, PartitionSpec as P

HEADS = 4
BLK = 128
EPSILON = 1e-05
GELU_COEF = math.sqrt(2.0 / math.pi)

AXES = ("x_hi", "core", "z", "x_lo", "y")
SIZES = (2, 2, 4, 2, 4)
ROOM = ("x_hi", "core")
GEOM = ("z", "x_lo", "y")
VMEM = pl.BlockSpec(memory_space=pltpu.VMEM)
SMEM = pl.BlockSpec(memory_space=pltpu.SMEM)
ANY = pl.BlockSpec(memory_space=pl.ANY)
FAR = 2
ORDER = (2, 1, 3)


def pairs_of(move):
    pairs = []
    for source in range(math.prod(SIZES)):
        target = move(*(int(i) for i in np.unravel_index(source, SIZES)))
        pairs.append((source, int(np.ravel_multi_index(target, SIZES))))
    return pairs


SWAP = pairs_of(lambda xh, c, z, xl, y: (xh, xl, z, c, y))
CORE = pairs_of(lambda xh, c, z, xl, y: (xh, 1 - c, z, xl, y))


def first(mask):
    return pairs_of(
        lambda xh, c, z, xl, y: (xh, c, z, xl, y ^ mask) if c == 0 else (xh, c, z ^ mask, xl, y)
    )


def first_swapped(mask):
    after = dict(first(mask))
    return [(source, after[target]) for source, target in SWAP]


def second(mask):
    return pairs_of(
        lambda xh, c, z, xl, y: (xh, c, z ^ mask, xl, y) if c == 0 else (xh, c, z, xl, y ^ mask)
    )


def along_x(mask):
    return pairs_of(lambda xh, c, z, xl, y: (xh ^ (mask >> 1), c, z, xl ^ (mask & 1), y))


def send(value, pairs):
    return lax.ppermute(value, AXES, pairs)


def normalize(inputs, gain):
    center = inputs - jnp.mean(inputs, axis=-1, keepdims=True)
    inverse = lax.rsqrt(jnp.mean(center * center, axis=-1, keepdims=True) + EPSILON)
    scaled = center * inverse
    return (scaled, inverse, scaled * gain)


def gelu_pair(inputs):
    inner = GELU_COEF * (inputs + 0.044715 * inputs * inputs * inputs)
    tangent = jnp.tanh(inner)
    value = 0.5 * inputs * (1.0 + tangent)
    slope = 0.5 * (1.0 + tangent) + 0.5 * inputs * (1.0 - tangent * tangent) * GELU_COEF * (
        1.0 + 3.0 * 0.044715 * inputs * inputs
    )
    return (value, slope)


def mult(left, right):
    return jnp.dot(left, right, preferred_element_type=jnp.float32)


def mult_nt(left, right):
    return lax.dot_general(
        left, right, (((1,), (1,)), ((), ())), preferred_element_type=jnp.float32
    )


def mult_tn(left, right):
    return lax.dot_general(
        left, right, (((0,), (0,)), ((), ())), preferred_element_type=jnp.float32
    )


def two_parts(value):
    high = value.astype(jnp.bfloat16)
    low = (value - high.astype(jnp.float32)).astype(jnp.bfloat16)
    return high, low


PARTS = 8
PIECES = 32
CHUNK = 128
TAIL = 16
LAYOUT = ((0, 16), (16, 16), (32, 16), (48, 16), (64, 16), (80, 16), (96, 32))


def lanes(value, combine):
    out = value[:, 0:BLK]
    for at in range(BLK, value.shape[1], BLK):
        out = combine(out, value[:, at : at + BLK])
    return out


def step_kernel(where, moved, seen, packed, w_up, w_down, gain_attn, gain_mlp, *refs):
    parts, (output, gains_out), refs = refs[:PARTS], refs[PARTS : PARTS + 2], refs[PARTS + 2 :]
    gives, keeps, refs = refs[:4], refs[4:8], refs[8:]
    scores, pulls, sums, stat, give, keep, tail, out_sems = refs
    f32, b16 = jnp.float32, jnp.bfloat16
    width = w_up.shape[0]
    w_query, w_key, w_value, w_out = (packed.at[pl.ds(i * width, width)] for i in range(4))
    head = width // HEADS
    factor = 1.0 / math.sqrt(head)
    cols = [slice(h * head, (h + 1) * head) for h in range(HEADS)]
    heads = [slice(h * BLK, (h + 1) * BLK) for h in range(HEADS)]
    inputs = moved[0:BLK, :].astype(f32)
    scaled_one, _, normed = normalize(inputs, gain_attn[...])
    normed_b = normed.astype(b16)
    query_rows = mult(normed_b, w_query[...]).astype(b16)

    blank = jnp.zeros((BLK, head), b16)
    query_pairs = jnp.concatenate(
        [
            jnp.concatenate(
                [query_rows[:, c] if h % 2 == side else blank for side in range(2)], axis=1
            )
            for h, c in enumerate(cols)
        ],
        axis=0,
    )
    pair_rows = [slice(0, 2 * BLK), slice(2 * BLK, 4 * BLK)]
    pair_cols = [slice(0, 2 * head), slice(2 * head, 4 * head)]

    stat[...] = jnp.full_like(stat, -1e30)

    for p in range(PARTS):
        key_rows = mult(parts[p][...], w_key[...]).astype(b16)
        allowed = seen[p : p + 1, :] > 0
        for r, c in zip(pair_rows, pair_cols):
            part = mult_nt(query_pairs[r, :], key_rows[:, c]) * factor
            part = jnp.where(allowed, part, -1e30)
            scores[p, r, :] = part
            stat[r, :] = jnp.maximum(stat[r, :], lanes(part, jnp.maximum))

    highest = jnp.max(stat[...], axis=-1, keepdims=True)
    stat[...] = jnp.zeros_like(stat)

    for p in range(PARTS):
        part = jnp.exp(scores[p] - highest)
        scores[p] = part
        stat[...] += lanes(part, jnp.add)

    inverse_sum = 1.0 / jnp.sum(stat[...], axis=-1, keepdims=True)
    sums[...] = jnp.zeros_like(sums)

    for p in range(PARTS):
        part = scores[p] * inverse_sum
        scores[p] = part
        sums[...] += mult(part.astype(b16), parts[p][...])

    u_high, u_low = two_parts(sums[...])
    context = jnp.concatenate(
        [mult(u_high[r], w_value[:, c]) + mult(u_low[r], w_value[:, c]) for r, c in zip(heads, cols)],
        axis=1,
    ).astype(b16)

    core = where[0]
    half = PIECES // 2

    def store(at, rows, grad):
        middle = grad.shape[0] // 2
        low, high = grad[:middle], grad[middle:]
        mine = jnp.where(core == 0, low, high).astype(b16)
        yours = jnp.where(core == 0, high, low).astype(b16)
        for i in range(half):
            row = i % 4 * CHUNK + at
            keep[i // 4, row : row + rows, :] = mine[i * rows : (i + 1) * rows]
            give[i // 4, row : row + rows, :] = yours[i * rows : (i + 1) * rows]

    mixed = inputs + mult(context, w_out[...])
    scaled_two, inverse_two, normed_two = normalize(mixed, gain_mlp[...])
    normed_two_b = normed_two.astype(b16)
    activated, slope = gelu_pair(mult(normed_two_b, w_up[...]))
    activated_b = activated.astype(b16)
    output[...] = (mixed + mult(activated_b, w_down[...])).astype(b16)
    cotangent = moved[BLK : 2 * BLK, :]
    store(96, 32, mult_tn(activated_b, cotangent))
    grad_upper_b = (mult_nt(cotangent, w_down[...]) * slope).astype(b16)
    store(64, 16, mult_tn(normed_two_b, grad_upper_b[:, :width]))
    store(80, 16, mult_tn(normed_two_b, grad_upper_b[:, width:]))
    grad_normed_two = mult_nt(grad_upper_b, w_up[...])
    grad_gain_mlp = jnp.sum(grad_normed_two * scaled_two, axis=0, keepdims=True)
    grad_scaled = grad_normed_two * gain_mlp[...]
    mean_one = jnp.mean(grad_scaled, axis=-1, keepdims=True)
    mean_two = jnp.mean(grad_scaled * scaled_two, axis=-1, keepdims=True)
    grad_mixed = cotangent.astype(f32) + inverse_two * (
        grad_scaled - mean_one - scaled_two * mean_two
    )
    grad_mixed_b = grad_mixed.astype(b16)
    store(48, 16, mult_tn(context, grad_mixed_b))
    grad_context = mult_nt(grad_mixed_b, w_out[...]).astype(b16)
    store(
        32,
        16,
        jnp.concatenate(
            [
                mult_tn(u_high[r], grad_context[:, c]) + mult_tn(u_low[r], grad_context[:, c])
                for r, c in zip(heads, cols)
            ],
            axis=1,
        ),
    )
    pulled = jnp.concatenate(
        [mult_nt(grad_context[:, c], w_value[:, c]) for c in cols], axis=0
    ).astype(b16)
    stat[...] = jnp.zeros_like(stat)

    for p in range(PARTS):
        part = mult_nt(pulled, parts[p][...])
        pulls[p] = part
        stat[...] += lanes(part * scores[p], jnp.add)

    centre = jnp.sum(stat[...], axis=-1, keepdims=True)
    sums[...] = jnp.zeros_like(sums)

    for p in range(PARTS):
        part = (scores[p] * (pulls[p] - centre) * factor).astype(b16)
        sums[...] += mult(part, parts[p][...])

    t_high, t_low = two_parts(sums[...])
    grad_query_rows = jnp.concatenate(
        [mult(t_high[r], w_key[:, c]) + mult(t_low[r], w_key[:, c]) for r, c in zip(heads, cols)],
        axis=1,
    ).astype(b16)
    store(
        16,
        16,
        jnp.concatenate(
            [
                mult_tn(t_high[r], query_rows[:, c]) + mult_tn(t_low[r], query_rows[:, c])
                for r, c in zip(heads, cols)
            ],
            axis=1,
        ),
    )
    store(0, 16, mult_tn(normed_b, grad_query_rows))
    grad_normed = mult_nt(grad_query_rows, w_query[...])
    grad_gain_attn = jnp.sum(grad_normed * scaled_one, axis=0, keepdims=True)
    gains = jnp.concatenate([grad_gain_attn, grad_gain_mlp, jnp.zeros((6, width), f32)], axis=0)
    put_gains(tail, 0, gains)
    gains_out[...] = gains
    one, two = where[1], where[2]
    copies = [
        pltpu.make_async_copy(tail, gives[FAR].at[pl.ds(4 * CHUNK, TAIL)], out_sems.at[8])
    ]
    for i, mask in enumerate(ORDER + (0,)):
        for j, (held, outs, index) in enumerate(((give, gives, two), (keep, keeps, one))):
            copies.append(
                pltpu.make_async_copy(
                    held.at[index ^ mask],
                    outs[mask].at[pl.ds(0, 4 * CHUNK)],
                    out_sems.at[2 * i + j],
                )
            )
    for copy in copies:
        copy.start()
    for copy in copies:
        copy.wait()


def device_step(where, moved, seen, parts, weights):
    f32, b16 = jnp.float32, jnp.bfloat16
    quarters = [(4 * CHUNK + (TAIL if mask == FAR else 0), 512) for mask in range(4)]
    return pl.pallas_call(
        step_kernel,
        out_shape=[
            jax.ShapeDtypeStruct((BLK, 512), b16),
            jax.ShapeDtypeStruct((8, 512), f32),
        ]
        + [jax.ShapeDtypeStruct(shape, b16) for shape in quarters]
        + [jax.ShapeDtypeStruct((4 * CHUNK, 512), b16)] * 4,
        in_specs=[SMEM] + [VMEM] * (7 + PARTS),
        out_specs=[VMEM] * 2 + [ANY] * 8,
        scratch_shapes=[
            pltpu.VMEM((PARTS, 512, 512), f32),
            pltpu.VMEM((PARTS, 512, 512), f32),
            pltpu.VMEM((512, 512), f32),
            pltpu.VMEM((512, BLK), f32),
            pltpu.VMEM((4, 4 * CHUNK, 512), b16),
            pltpu.VMEM((4, 4 * CHUNK, 512), b16),
            pltpu.VMEM((TAIL, 512), b16),
            pltpu.SemaphoreType.DMA((9,)),
        ],
        compiler_params=pltpu.CompilerParams(vmem_limit_bytes=38 << 20),
        cost_estimate=pl.CostEstimate(
            flops=12 * 10**9, bytes_accessed=18 * 10**6, transcendentals=3 * 10**6
        ),
    )(where, moved, seen, *weights, *parts)


def put_gains(ref, at, gains):
    high = gains.astype(jnp.bfloat16)
    low = (gains - high.astype(jnp.float32)).astype(jnp.bfloat16)
    ref[at : at + TAIL, :] = jnp.concatenate([high, low], axis=0)


def take_gains(ref, at):
    tail = ref[at : at + TAIL, :].astype(jnp.float32)
    return tail[: TAIL // 2] + tail[TAIL // 2 :]


def lift_far_kernel(keep, arrived, gains_ref, give, gains_out):
    rows = keep.shape[0]
    total = keep[...].astype(jnp.float32) + arrived[0:rows, :].astype(jnp.float32)
    give[0:rows, :] = total.astype(jnp.bfloat16)
    gains = add_gains(gains_ref[...], [take_gains(arrived, rows)])
    put_gains(give, rows, gains)
    gains_out[...] = gains


def lift_kernel(keep, arrived, gains_ref, give):
    rows = keep.shape[0]
    total = keep[...].astype(jnp.float32) + arrived[...].astype(jnp.float32)
    give[0:rows, :] = total.astype(jnp.bfloat16)
    put_gains(give, rows, gains_ref[...])


def quarters_kernel(where, keep, across, gains_ref, *refs):
    arrived, gives, own, gains_out = refs[:3], refs[3:6], refs[6], refs[7]
    for mask in range(4):
        at = pl.ds(pl.multiple_of((where[2] ^ mask) * CHUNK, CHUNK), CHUNK)
        value = keep[at, :].astype(jnp.float32) + across[at, :].astype(jnp.float32)
        for ref in arrived:
            value = value + ref[at, :].astype(jnp.float32)
        if mask:
            gives[mask - 1][0:CHUNK, :] = value.astype(jnp.bfloat16)
        else:
            own[...] = value
    gains = add_gains(gains_ref[...], [take_gains(ref, 4 * CHUNK) for ref in arrived])
    for give in gives:
        put_gains(give, CHUNK, gains)
    gains_out[...] = gains


def add_gains(own, arrived):
    high = own.astype(jnp.bfloat16).astype(jnp.float32)
    own = high + (own - high).astype(jnp.bfloat16).astype(jnp.float32)
    if len(arrived) == 1:
        return own + arrived[0]
    return (own + arrived[0]) + (arrived[1] + arrived[2])


def chunk_kernel(own_ref, gains_ref, *refs):
    arrived, give = refs[:3], refs[3]
    rows = own_ref.shape[0]
    value = own_ref[...]
    for ref in arrived:
        value = value + ref[0:rows, :].astype(jnp.float32)
    give[0:rows, :] = value.astype(jnp.bfloat16)
    put_gains(give, rows, add_gains(gains_ref[...], [take_gains(ref, rows) for ref in arrived]))


def last_kernel(own_ref, *refs):
    arrived, chunk, gains = refs[:3], refs[3], refs[4]
    rows = chunk.shape[0]
    a, b, c, d = (ref[0:rows, :].astype(jnp.float32) for ref in (own_ref, *arrived))
    chunk[...] = ((a + b) + (c + d)).astype(jnp.bfloat16)
    a, b, c, d = (take_gains(ref, rows) for ref in (own_ref, *arrived))
    put_gains(gains, 0, (a + b) + (c + d))


def arrange_kernel(where, gains, *refs):
    chunks, out = refs[:4], refs[4]
    for mask, chunk in enumerate(chunks):
        for at, rows in LAYOUT:
            to = pl.multiple_of(at * 4 + (where[2] ^ mask) * rows, 16)
            out[pl.ds(to, rows), :] = chunk[at : at + rows, :]
    out[4 * CHUNK :, :] = gains[...]


def place_kernel(where, *refs):
    groups, refs = (refs[0:4], refs[4:8]), refs[8:]
    output, output_out, outs, gain_attn, gain_mlp = refs[0], refs[1], refs[2:8], refs[8], refs[9]
    grads, sems = refs[10:16], refs[16]
    output_out[0] = output[...]
    copies = []
    for j, (at, rows) in enumerate(LAYOUT):
        i = min(j, 4) if j < 6 else 5
        for side, group in enumerate(groups):
            holder = where[0] ^ side
            for mask, arranged in enumerate(group):
                part = holder * 4 + (where[1 + side] ^ mask)
                to = pl.ds(pl.multiple_of(part * (4 * rows), 64), 4 * rows)
                piece = arranged[at * 4 : (at + rows) * 4, :]
                if j in (4, 5):
                    grads[4][to, 512 * (j - 4) : 512 * (j - 3)] = piece
                else:
                    grads[i][to, :] = piece
        if j != 4:
            copies.append(pltpu.make_async_copy(grads[i], outs[i], sems.at[i]))
            copies[-1].start()
    own, other = (take_gains(group[0], 4 * CHUNK) for group in groups)
    gains = jnp.where(where[0] == 0, own, other).astype(jnp.bfloat16)
    gain_attn[...] = gains[0]
    gain_mlp[...] = gains[1]
    for copy in copies:
        copy.wait()


def call(kernel, outs, *operands, scalars=0):
    return pl.pallas_call(
        kernel,
        out_shape=[jax.ShapeDtypeStruct(shape, dtype) for shape, dtype in outs],
        in_specs=[SMEM] * scalars + [VMEM] * (len(operands) - scalars),
        out_specs=[VMEM] * len(outs),
        compiler_params=pltpu.CompilerParams(vmem_limit_bytes=24 << 20),
    )(*operands)


def to_peers(give_of, route):
    return dict(sorted((mask, send(give_of(mask), route(mask))) for mask in ORDER))


def sum_everywhere(where, output, gains, *quarters):
    gives, keeps = quarters[:4], quarters[4:]
    b16, f32 = jnp.bfloat16, jnp.float32
    message = ((4 * CHUNK + TAIL, 512), b16)

    across = {mask: send(gives[mask], CORE) for mask in ORDER + (0,)}
    far, gains = call(lift_far_kernel, [message, ((8, 512), f32)], keeps[FAR], across[FAR], gains)

    def lifted(mask):
        if mask == FAR:
            return far
        return call(lift_kernel, [message], keeps[mask], across[mask], gains)[0]

    arrived = to_peers(lifted, first).values()
    output, *arrived = lax.optimization_barrier((send(output, SWAP), *arrived))
    small = ((CHUNK + TAIL, 512), b16)
    *gives, own, gains = call(
        quarters_kernel,
        [small] * 3 + [((CHUNK, 512), f32), ((8, 512), f32)],
        where, keeps[0], across[0], gains, *arrived, scalars=1,
    )
    arrived = to_peers(lambda mask: gives[mask - 1], second).values()
    (give,) = call(chunk_kernel, [small], own, gains, *arrived)
    arrived = to_peers(lambda mask: give, along_x).values()
    chunk, gains = call(last_kernel, [((CHUNK, 512), b16), ((TAIL, 512), b16)], give, *arrived)

    chunks = [chunk, *to_peers(lambda mask: chunk, second).values()]
    (mine,) = call(arrange_kernel, [message], where, gains, *chunks, scalars=1)
    own = {0: mine, **to_peers(lambda mask: mine, first)}
    other = {mask: send(own[mask], CORE) for mask in (0,) + ORDER}
    shapes = [(512, 512)] * 4 + [(512, 1024), (1024, 512)]
    outs = [(1, BLK, 512), *shapes, (512,), (512,)]
    placed = pl.pallas_call(
        place_kernel,
        out_shape=[jax.ShapeDtypeStruct(shape, b16) for shape in outs],
        in_specs=[SMEM] + [VMEM] * 9,
        out_specs=[VMEM] + [ANY] * 6 + [VMEM] * 2,
        scratch_shapes=[pltpu.VMEM(shape, b16) for shape in shapes]
        + [pltpu.SemaphoreType.DMA((6,))],
        compiler_params=pltpu.CompilerParams(vmem_limit_bytes=24 << 20),
    )(where, *(own[mask] for mask in range(4)), *(other[mask] for mask in range(4)), output)
    return tuple(placed)


def gather_features(own, others, seen, weights):
    near = {mask: send(own, first_swapped(mask)) for mask in (0,) + ORDER}
    mine = jnp.concatenate([near[mask] for mask in range(4)])
    mine, others, seen, weights = lax.optimization_barrier((mine, others, seen, weights))
    group = [mine, *to_peers(lambda mask: mine, second).values()]
    parts = group + [send(part, CORE) for part in group]
    core, y, z = (lax.axis_index(name) for name in ("core", "y", "z"))
    side, two, one = (jnp.asarray(i) for i in np.unravel_index(np.arange(32), (2, 4, 4)))
    holder = core ^ side
    block_y = jnp.where(holder == 0, y ^ one, y ^ two)
    block_z = jnp.where(holder == 0, z ^ two, z ^ one)
    others = jnp.concatenate([*others, jnp.pad(seen, ((0, 15), (0, 512 - seen.shape[-1])))])
    return parts, block_z * 8 + holder * 4 + block_y, send(others, SWAP), jnp.concatenate(weights)


def local(
    queries,
    features,
    visible,
    cotangent,
    w_query,
    w_key,
    w_value,
    w_out,
    w_up,
    w_down,
    gain_attn,
    gain_mlp,
):
    parts, blocks, moved, packed = gather_features(
        features[0],
        (queries[0], cotangent[0]),
        visible[0].astype(jnp.bfloat16),
        (w_query, w_key, w_value, w_out),
    )
    seen = jnp.take(moved[2 * BLK].astype(jnp.float32), blocks)
    core, y, z = (lax.axis_index(name).astype(jnp.int32) for name in ("core", "y", "z"))
    where = jnp.stack([core, jnp.where(core == 0, y, z), jnp.where(core == 0, z, y)])
    return sum_everywhere(
        where,
        *device_step(
            where,
            moved,
            jnp.repeat(seen, BLK).reshape(PARTS, 512),
            parts,
            (packed, w_up, w_down, gain_attn[None], gain_mlp[None]),
        )
    )


def solution(mesh):
    parts = Mesh(mesh.devices.reshape(SIZES), AXES)
    split = P(ROOM, GEOM, None)
    return jax.shard_map(
        local,
        mesh=parts,
        in_specs=(split,) * 4 + (P(),) * 8,
        out_specs=(split,) + (P(),) * 8,
        check_vma=False,
    )
```
